256 devices in a mesh: seq: 64 (over x, z_hi, y, core), chan: 4 (over z_lo).
Axes of the slice: x: 4, y: 4, z: 8 (z_hi: 2, z_lo: 4; z = z_hi * 4 + z_lo), core: 2. Of those that a mesh axis runs over, the one named last changes fastest.
Arguments:
- signal: bfloat16 [1024, 16384], P('chan', 'seq'), may hold values from -6 to 6
- gating: bfloat16 [1024, 16384], P('chan', 'seq'), may hold values from -6 to 6
- filter_taps: float32 [1024, 16384], P('chan', 'seq'), may hold values from -6 to 6
- decay_rates: float32 [1024], P('chan'), may hold values from 1.5258789e-05 to 0.0009765625
- out_weight: bfloat16 [1024, 2048], P(None, 'chan'), may hold values from -0.1875 to 0.1875
- out_grad: bfloat16 [16384, 2048], P('seq', 'chan'), may hold values from -1.5 to 1.5
Outputs:
- mixed_out: bfloat16 [16384, 2048], P('seq', 'chan')
- signal_grad: float32 [1024, 16384], P('chan', 'seq')
- gating_grad: float32 [1024, 16384], P('chan', 'seq')
- taps_grad: float32 [1024, 16384], P('chan', 'seq')
The draws below stay inside these ranges and needn't reach their ends.
All inputs are finite; a program needn't handle non-finite values.
Results may differ from the reference program's by a relative error of at most 0.013.
Values may be sent and summed in bfloat16 or wider, within the bound.
A program may use at most 64 MiB of HBM per device.

```python
import math
import jax
import jax.numpy as jnp
from jax import lax

CH = 1024
DM = 2048
LEN = 16384


def steps_of(stream_key, extent, cuts, smallest, high):
    def one(axis_at, blocks):
        heights = jax.random.uniform(jax.random.fold_in(jax.random.fold_in(stream_key, 6), axis_at), (blocks,), jnp.float32, smallest / len(cuts), high / len(cuts))
        return jnp.repeat(jnp.exp(heights), extent[axis_at] // blocks).reshape((-1,) + (1,) * (len(extent) - axis_at - 1))

    factor_of = one(*cuts[0])
    for cut in cuts[1:]:
        factor_of = factor_of * one(*cut)
    return factor_of


def bell_draw(key, shape, spread, most, cuts=(), held_as=jnp.bfloat16):
    factor_of = steps_of(key, shape, cuts, -0.22, 0.18) if cuts else 1.0
    array = jax.random.normal(key, shape, jnp.float32) * spread * factor_of
    return jnp.minimum(jnp.maximum(array, -most), most).astype(held_as)


def setup_inputs(seed: int = 0) -> dict:
    arg_keys = jax.random.split(jax.random.key(seed), 7)
    return {
        "signal": bell_draw(arg_keys[0], (CH, LEN), 1.0, 6.0, ((0, 4), (1, 64))),
        "gating": bell_draw(arg_keys[1], (CH, LEN), 1.0, 6.0, ((0, 4), (1, 64))),
        "filter_taps": bell_draw(arg_keys[2], (CH, LEN), 1.0, 6.0, ((0, 4), (1, 64)), jnp.float32),
        "decay_rates": jnp.clip(jnp.exp(math.log(0.0009765625) - 4.158883 * jax.random.uniform(arg_keys[3], (CH,), jnp.float32) ** steps_of(arg_keys[3], (CH,), ((0, 4),), -0.2, 0.2)), 1.52587890625e-05, 0.0009765625),
        "out_weight": bell_draw(arg_keys[4], (CH, DM), CH ** -0.5, 0.1875, ((1, 4),)),
        "out_grad": bell_draw(arg_keys[5], (LEN, DM), 0.25, 1.5, ((0, 64), (1, 4))),
    }


def reference(signal, gating, filter_taps, decay_rates, out_weight, out_grad):
    length = signal.shape[1]
    fft_length = 2 * length
    places = jnp.arange(length, dtype=jnp.int32).astype(jnp.float32)
    window = jnp.exp(-decay_rates[:, None] * places[None, :]) * jnp.sqrt(2.0 * decay_rates)[:, None]
    filters = filter_taps * window
    inputs = signal.astype(jnp.float32)

    def convolve(operands):
        first_row, second_row = operands
        product = jnp.fft.rfft(first_row, n=fft_length) * jnp.fft.rfft(second_row, n=fft_length)
        return jnp.fft.irfft(product, n=fft_length)[:length]

    def correlate(operands):
        first_row, second_row = operands
        product = jnp.fft.rfft(first_row, n=fft_length) * jnp.conj(jnp.fft.rfft(second_row, n=fft_length))
        return jnp.fft.irfft(product, n=fft_length)[:length]
    mixed = lax.map(convolve, (inputs, filters))
    gate_values = gating.astype(jnp.float32)
    gated_rows = (gate_values * mixed).astype(jnp.bfloat16)
    mixed_out = jnp.dot(gated_rows.T, out_weight, preferred_element_type=jnp.float32).astype(jnp.bfloat16)
    grad_mixed_out = jnp.dot(out_weight, out_grad.T, preferred_element_type=jnp.float32)
    gating_grad = grad_mixed_out * mixed
    grad_mixed = grad_mixed_out * gate_values
    signal_grad = lax.map(correlate, (grad_mixed, filters))
    taps_grad = lax.map(correlate, (grad_mixed, inputs)) * window
    return (mixed_out, signal_grad, gating_grad, taps_grad)
```

```python
import functools

import jax
import jax.numpy as jnp
import numpy as np
from jax import lax
from jax.experimental import pallas as pl
from jax.experimental.pallas import tpu as pltpu
from jax.sharding import PartitionSpec as P

F32, BF16 = jnp.float32, jnp.bfloat16
MESH = pl.DeviceIdType.MESH
LANES = 128


def halves(table):
    high = table.astype(BF16)
    return high, (table - high.astype(np.float64)).astype(BF16)


def tables(shards, folds):
    rows = shards * folds
    length = rows * LANES
    freq = 2 * np.arange(rows)[:, None] + 1
    order = np.arange(rows)
    coarse = folds * (order % shards) + order // shards
    angle = 2 * np.pi * (freq * coarse[None, :] % (4 * rows)) / (4 * rows)
    first = np.concatenate([np.cos(angle), -np.sin(angle)], 0)
    fine = np.arange(LANES)
    turn = 2 * np.pi * (freq * fine[None, :]) / (4 * length)
    inner = 2 * np.pi * (fine[:, None] * fine[None, :] % LANES) / LANES
    re, im = np.cos(inner), -np.sin(inner)
    ahead = np.block([[re, im], [-im, re]])
    back = np.block([[re, -im], [im, re]])
    first_high, first_low = halves(first)
    last_high, last_low = halves(first.T / length)
    return (
        np.concatenate([first_high, first_low], 1),
        last_high,
        last_low,
        *halves(ahead),
        *halves(back),
        np.cos(turn).astype(np.float32),
        (-np.sin(turn)).astype(np.float32),
    )


def split(value):
    high = value.astype(BF16)
    return high, (value - high.astype(F32)).astype(BF16)


def mm(left, right):
    return jnp.dot(left, right, preferred_element_type=F32)


def body(
    shards, chans,
    sig_ref, gate_ref, taps_ref, decay_ref, weight_ref, og_ref,
    first_ref, lasth_ref, lastl_ref, fwdh_ref, fwdl_ref, bckh_ref, bckl_ref, cos_ref, sin_ref,
    out_ref, sgrad_ref, ggrad_ref, tgrad_ref,
    in_send, in_recv, rs_send, rs_recv, mx_send, mx_recv, gr_send, gr_recv, rt_send, rt_recv, ag_send, ag_recv,
    rows, window, grad_out, xcat, bh, bl, spec, zh, zl,
    sends, recvs,
):
    me, ch = lax.axis_index("seq"), lax.axis_index("chan")
    far = lax.rem(ch + chans // 2, chans)
    wide, span = sig_ref.shape
    folds = span // LANES
    mine = wide // shards
    n1 = shards * folds

    barrier = pltpu.get_barrier_semaphore()

    @pl.loop(0, shards)
    def _(i):
        pl.semaphore_signal(barrier, inc=1, device_id=(i, far), device_id_type=MESH)

    near = [k for k in range(1, chans) if k != chans // 2]
    for k in near:
        pl.semaphore_signal(barrier, inc=1, device_id=(me, lax.rem(ch + k, chans)), device_id_type=MESH)

    def to_rows(value):
        for h in range(folds):
            rows[pl.ds(h, wide, stride=folds), :] = value[:, h * LANES : (h + 1) * LANES]
        return rows[...].reshape(shards, mine * folds, LANES).astype(BF16)

    def from_rows(block):
        rows[...] = block.astype(F32).reshape(wide * folds, LANES)
        return [rows[pl.ds(h, wide, stride=folds), :] for h in range(folds)]

    def spread(source, target, k):
        @pl.loop(0, shards)
        def _(i):
            peer = lax.rem(me + i, shards)
            pltpu.make_async_remote_copy(
                source.at[peer], target.at[me], sends.at[k], recvs.at[k],
                device_id=(peer, far), device_id_type=MESH,
            ).start()

    def joint(source, target, k):
        return pltpu.make_async_remote_copy(
            source, target, sends.at[k], recvs.at[k], device_id=(me, far), device_id_type=MESH
        )

    place = lax.broadcasted_iota(jnp.int32, (1, span), 1) + me * span
    place = place.astype(F32)
    for i in range(wide // LANES):
        row = decay_ref[i : i + 1, :]
        rate = jnp.transpose(jnp.broadcast_to(row, (LANES, LANES)))
        size = jnp.sqrt(2.0 * rate)
        for h in range(folds):
            cols = slice(h * LANES, (h + 1) * LANES)
            window[i * LANES : (i + 1) * LANES, cols] = jnp.exp(-rate * place[:, cols]) * size

    in_send[:, 0] = to_rows(sig_ref[...].astype(F32))
    in_send[:, 1] = to_rows(taps_ref[...] * window[...])

    pl.semaphore_wait(barrier, shards + len(near))
    spread(in_send, in_recv, 0)

    def share(k):
        block = lax.rem(ch + k, chans)
        part = weight_ref[pl.ds(pl.multiple_of(block * wide, wide), wide), :]
        return lax.dot_general(part, og_ref[...], (((1,), (1,)), ((), ())), preferred_element_type=F32)

    for k in range(1, chans):
        rs_send[k - 1] = share(k).astype(BF16)
        pltpu.make_async_remote_copy(
            rs_send.at[k - 1], rs_recv.at[k - 1], sends.at[1], recvs.at[1],
            device_id=(me, lax.rem(ch + k, chans)), device_id_type=MESH,
        ).start()
    grad_out[...] = share(0).astype(BF16).astype(F32)

    cosine, sine = cos_ref[...], sin_ref[...]

    def analyse(block, base):
        rows[...] = block.astype(F32).reshape(wide * folds, LANES)
        for c in range(mine):
            column = jnp.concatenate(
                [rows[pl.ds(c * folds + h, shards, stride=mine * folds), :] for h in range(folds)], 0
            ).astype(BF16)
            cols = slice(c * LANES, (c + 1) * LANES)
            xcat[:n1, cols] = column
            xcat[n1:, cols] = column
        stage = mm(first_ref[...], xcat[...])
        for c in range(mine):
            cols = slice(c * LANES, (c + 1) * LANES)
            real, imag = stage[:n1, cols], stage[n1:, cols]
            turned = jnp.concatenate([real * cosine - imag * sine, real * sine + imag * cosine], 1)
            bh[c * n1 : (c + 1) * n1], bl[c * n1 : (c + 1) * n1] = split(turned)
        high, low = bh[...], bl[...]
        spec[base] = mm(high, fwdh_ref[...]) + mm(low, fwdh_ref[...]) + mm(high, fwdl_ref[...])

    def synthesize(real, imag):
        high, low = split(jnp.concatenate([real, imag], 1))
        stage = mm(high, bckh_ref[...]) + mm(low, bckh_ref[...]) + mm(high, bckl_ref[...])
        for c in range(mine):
            part = stage[c * n1 : (c + 1) * n1]
            real, imag = part[:, :LANES], part[:, LANES:]
            turned = jnp.concatenate([real * cosine + imag * sine, imag * cosine - real * sine], 0)
            cols = slice(c * LANES, (c + 1) * LANES)
            zh[:, cols], zl[:, cols] = split(turned)
        high, low = zh[...], zl[...]
        result = mm(lasth_ref[...], high) + mm(lasth_ref[...], low) + mm(lastl_ref[...], high)
        for c in range(mine):
            for h in range(folds):
                rows[pl.ds(c * folds + h, shards, stride=mine * folds), :] = result[
                    h * shards : (h + 1) * shards, c * LANES : (c + 1) * LANES
                ]
        return rows[...].reshape(shards, mine * folds, LANES).astype(BF16)

    def parts(k):
        return spec[k, :, :LANES], spec[k, :, LANES:]

    joint(in_send, in_recv, 0).wait_recv()
    analyse(in_recv[:, 0], 0)
    analyse(in_recv[:, 1], 1)
    (sr, si), (fr, fi) = parts(0), parts(1)
    mx_send[...] = synthesize(sr * fr - si * fi, sr * fi + si * fr)
    spread(mx_send, mx_recv, 2)

    joint(rs_send, rs_recv, 1).wait_recv()
    total = grad_out[...]
    for k in range(chans - 1):
        total = total + rs_recv[k].astype(F32)
    grad_out[...] = total
    gr_send[...] = to_rows(total * gate_ref[...].astype(F32))
    spread(gr_send, gr_recv, 3)

    joint(mx_send, mx_recv, 2).wait_recv()
    mixed = jnp.concatenate(from_rows(mx_recv[...]), 1)
    ag_send[...] = jnp.transpose(mixed * gate_ref[...].astype(F32)).astype(BF16)
    for k in range(1, chans):
        pltpu.make_async_remote_copy(
            ag_send, ag_recv.at[k - 1], sends.at[4], recvs.at[4],
            device_id=(me, lax.rem(ch + k, chans)), device_id_type=MESH,
        ).start()
    ggrad_ref[...] = grad_out[...] * mixed

    joint(gr_send, gr_recv, 3).wait_recv()
    analyse(gr_recv[...], 2)
    gr, gi = parts(2)
    fr, fi = parts(1)
    rt_send[:, 0] = synthesize(gr * fr + gi * fi, gi * fr - gr * fi)
    sr, si = parts(0)
    gr, gi = parts(2)
    rt_send[:, 1] = synthesize(gr * sr + gi * si, gi * sr - gr * si)
    spread(rt_send, rt_recv, 5)

    def project(block, gathered):
        part = weight_ref[pl.ds(pl.multiple_of(block * wide, wide), wide), :]
        return mm(gathered, part)

    joint(ag_recv, ag_recv, 4).wait_recv()
    total = project(ch, ag_send[...])
    for k in range(1, chans):
        total = total + project(lax.rem(ch + chans - k, chans), ag_recv[k - 1])
    out_ref[...] = total.astype(BF16)

    joint(rt_send, rt_recv, 5).wait_recv()
    for h, value in enumerate(from_rows(rt_recv[:, 0])):
        sgrad_ref[:, h * LANES : (h + 1) * LANES] = value
    for h, value in enumerate(from_rows(rt_recv[:, 1])):
        cols = slice(h * LANES, (h + 1) * LANES)
        tgrad_ref[:, cols] = value * window[:, cols]

    joint(in_send, in_recv, 0).wait_send()
    joint(rs_send, rs_recv, 1).wait_send()
    joint(mx_send, mx_recv, 2).wait_send()
    joint(gr_send, gr_recv, 3).wait_send()
    joint(ag_recv, ag_recv, 4).wait_send()
    joint(rt_send, rt_recv, 5).wait_send()


def per_device(shards, chans, consts, signal, gating, filter_taps, decay_rates, out_weight, out_grad):
    wide, span = signal.shape
    folds = span // LANES
    mine = wide // shards
    n1 = shards * folds
    tile = (mine * folds, LANES)
    vmem = pl.BlockSpec(memory_space=pltpu.VMEM)
    return pl.pallas_call(
        functools.partial(body, shards, chans),
        out_shape=(
            jax.ShapeDtypeStruct(out_grad.shape, BF16),
            jax.ShapeDtypeStruct(signal.shape, F32),
            jax.ShapeDtypeStruct(signal.shape, F32),
            jax.ShapeDtypeStruct(signal.shape, F32),
        ),
        in_specs=[vmem] * (6 + len(consts)),
        out_specs=(vmem,) * 4,
        scratch_shapes=[
            pltpu.VMEM((shards, 2, *tile), BF16),
            pltpu.VMEM((shards, 2, *tile), BF16),
            pltpu.VMEM((chans - 1, wide, span), BF16),
            pltpu.VMEM((chans - 1, wide, span), BF16),
            pltpu.VMEM((shards, *tile), BF16),
            pltpu.VMEM((shards, *tile), BF16),
            pltpu.VMEM((shards, *tile), BF16),
            pltpu.VMEM((shards, *tile), BF16),
            pltpu.VMEM((shards, 2, *tile), BF16),
            pltpu.VMEM((shards, 2, *tile), BF16),
            pltpu.VMEM((span, wide), BF16),
            pltpu.VMEM((chans - 1, span, wide), BF16),
            pltpu.VMEM((wide * folds, LANES), F32),
            pltpu.VMEM((wide, span), F32),
            pltpu.VMEM((wide, span), F32),
            pltpu.VMEM((2 * n1, mine * LANES), BF16),
            pltpu.VMEM((mine * n1, 2 * LANES), BF16),
            pltpu.VMEM((mine * n1, 2 * LANES), BF16),
            pltpu.VMEM((3, mine * n1, 2 * LANES), F32),
            pltpu.VMEM((2 * n1, mine * LANES), BF16),
            pltpu.VMEM((2 * n1, mine * LANES), BF16),
            pltpu.SemaphoreType.DMA((6,)),
            pltpu.SemaphoreType.DMA((6,)),
        ],
        compiler_params=pltpu.CompilerParams(collective_id=0, has_side_effects=True, vmem_limit_bytes=48 << 20),
    )(
        signal, gating, filter_taps, decay_rates.reshape(-1, LANES), out_weight, out_grad, *map(jnp.asarray, consts)
    )


def solution(mesh):
    shards, chans = mesh.shape["seq"], mesh.shape["chan"]

    def step(signal, gating, filter_taps, decay_rates, out_weight, out_grad):
        consts = tables(shards, signal.shape[1] // shards // LANES)
        return jax.shard_map(
            functools.partial(per_device, shards, chans, consts),
            mesh=mesh,
            in_specs=(
                P("chan", "seq"),
                P("chan", "seq"),
                P("chan", "seq"),
                P("chan"),
                P(None, "chan"),
                P("seq", "chan"),
            ),
            out_specs=(P("seq", "chan"), P("chan", "seq"), P("chan", "seq"), P("chan", "seq")),
            check_vma=False,
        )(signal, gating, filter_taps, decay_rates, out_weight, out_grad)

    return step
```

```python
import functools

import jax
import jax.numpy as jnp
import numpy as np
from jax import lax
from jax.experimental import pallas as pl
from jax.experimental.pallas import tpu as pltpu
from jax.sharding import PartitionSpec as P

F32, BF16 = jnp.float32, jnp.bfloat16
MESH = pl.DeviceIdType.MESH
LANES = 128


def halves(table):
    high = table.astype(BF16)
    return high, (table - high.astype(np.float64)).astype(BF16)


def tables(shards, folds):
    rows = shards * folds
    length = rows * LANES
    freq = 2 * np.arange(rows)[:, None] + 1
    order = np.arange(rows)
    coarse = folds * (order % shards) + order // shards
    angle = 2 * np.pi * (freq * coarse[None, :] % (4 * rows)) / (4 * rows)
    first = np.concatenate([np.cos(angle), -np.sin(angle)], 0)
    fine = np.arange(LANES)
    turn = 2 * np.pi * (freq * fine[None, :]) / (4 * length)
    inner = 2 * np.pi * (fine[:, None] * fine[None, :] % LANES) / LANES
    re, im = np.cos(inner), -np.sin(inner)
    ahead = np.block([[re, im], [-im, re]])
    back = np.block([[re, -im], [im, re]])
    first_high, first_low = halves(first)
    last_high, last_low = halves(first.T / length)
    return (
        np.stack([np.concatenate([first_high, first_low], 1), *halves(ahead), *halves(back)]),
        np.stack([last_high, last_low]),
        np.stack([np.cos(turn), -np.sin(turn)]).astype(np.float32),
    )


def split(value):
    high = value.astype(BF16)
    return high, (value - high.astype(F32)).astype(BF16)


def mm(left, right):
    return jnp.dot(left, right, preferred_element_type=F32)


def body(
    shards, chans,
    sig_hbm, gate_hbm, taps_hbm, decay_hbm, weight_hbm, og_hbm, square_hbm, last_hbm, turn_hbm,
    out_ref, sgrad_ref, ggrad_ref, tgrad_ref,
    in_send, in_recv, rs_send, rs_recv, mx_send, mx_recv, gr_send, gr_recv, rt_send, rt_recv, ag_send, ag_recv,
    rows, window, grad_out, xcat, bh, bl, spec, zh, zl,
    sig_ref, gate_ref, taps_ref, decay_ref, weight_ref, og_ref, square_ref, last_ref, turn_ref,
    sends, recvs, loads,
):
    me, ch = lax.axis_index("seq"), lax.axis_index("chan")
    far = lax.rem(ch + chans // 2, chans)
    wide, span = sig_ref.shape
    folds = span // LANES
    mine = wide // shards
    n1 = shards * folds

    arrivals = [
        pltpu.make_async_copy(source, target, loads.at[k])
        for k, (source, target) in enumerate(
            (
                (sig_hbm, sig_ref), (taps_hbm, taps_ref), (og_hbm, og_ref), (weight_hbm, weight_ref),
                (square_hbm, square_ref), (last_hbm, last_ref), (turn_hbm, turn_ref), (gate_hbm, gate_ref), (decay_hbm, decay_ref),
            )
        )
    ]
    for k in (8, 0, 1, 2, 3, 4, 5, 6, 7):
        arrivals[k].start()
    first_ref, fwdh_ref, fwdl_ref, bckh_ref, bckl_ref = (square_ref.at[k] for k in range(5))
    lasth_ref, lastl_ref = last_ref.at[0], last_ref.at[1]

    barrier = pltpu.get_barrier_semaphore()

    @pl.loop(0, shards)
    def _(i):
        pl.semaphore_signal(barrier, inc=1, device_id=(i, far), device_id_type=MESH)

    near = [k for k in range(1, chans) if k != chans // 2]
    for k in near:
        pl.semaphore_signal(barrier, inc=1, device_id=(me, lax.rem(ch + k, chans)), device_id_type=MESH)

    def to_rows(value):
        for h in range(folds):
            rows[pl.ds(h, wide, stride=folds), :] = value[:, h * LANES : (h + 1) * LANES]
        return rows[...].reshape(shards, mine * folds, LANES).astype(BF16)

    def from_rows(block):
        rows[...] = block.astype(F32).reshape(wide * folds, LANES)
        return [rows[pl.ds(h, wide, stride=folds), :] for h in range(folds)]

    def spread(source, target, k):
        @pl.loop(0, shards)
        def _(i):
            peer = lax.rem(me + i, shards)
            pltpu.make_async_remote_copy(
                source.at[peer], target.at[me], sends.at[k], recvs.at[k],
                device_id=(peer, far), device_id_type=MESH,
            ).start()

    def joint(source, target, k):
        return pltpu.make_async_remote_copy(
            source, target, sends.at[k], recvs.at[k], device_id=(me, far), device_id_type=MESH
        )

    arrivals[8].wait()
    place = lax.broadcasted_iota(jnp.int32, (1, span), 1) + me * span
    place = place.astype(F32)
    for i in range(wide // LANES):
        row = decay_ref[i : i + 1, :]
        rate = jnp.transpose(jnp.broadcast_to(row, (LANES, LANES)))
        size = jnp.sqrt(2.0 * rate)
        for h in range(folds):
            cols = slice(h * LANES, (h + 1) * LANES)
            window[i * LANES : (i + 1) * LANES, cols] = jnp.exp(-rate * place[:, cols]) * size

    arrivals[0].wait()
    arrivals[1].wait()
    in_send[:, 0] = to_rows(sig_ref[...].astype(F32))
    in_send[:, 1] = to_rows(taps_ref[...] * window[...])

    pl.semaphore_wait(barrier, shards + len(near))
    spread(in_send, in_recv, 0)

    arrivals[2].wait()
    arrivals[3].wait()

    def share(k):
        block = lax.rem(ch + k, chans)
        part = weight_ref[pl.ds(pl.multiple_of(block * wide, wide), wide), :]
        return lax.dot_general(part, og_ref[...], (((1,), (1,)), ((), ())), preferred_element_type=F32)

    for k in range(1, chans):
        rs_send[k - 1] = share(k).astype(BF16)
        pltpu.make_async_remote_copy(
            rs_send.at[k - 1], rs_recv.at[k - 1], sends.at[1], recvs.at[1],
            device_id=(me, lax.rem(ch + k, chans)), device_id_type=MESH,
        ).start()
    grad_out[...] = share(0).astype(BF16).astype(F32)

    for arrival in arrivals[4:8]:
        arrival.wait()
    cosine, sine = turn_ref[0], turn_ref[1]

    def analyse(block, base):
        rows[...] = block.astype(F32).reshape(wide * folds, LANES)
        for c in range(mine):
            column = jnp.concatenate(
                [rows[pl.ds(c * folds + h, shards, stride=mine * folds), :] for h in range(folds)], 0
            ).astype(BF16)
            cols = slice(c * LANES, (c + 1) * LANES)
            xcat[:n1, cols] = column
            xcat[n1:, cols] = column
        stage = mm(first_ref[...], xcat[...])
        for c in range(mine):
            cols = slice(c * LANES, (c + 1) * LANES)
            real, imag = stage[:n1, cols], stage[n1:, cols]
            turned = jnp.concatenate([real * cosine - imag * sine, real * sine + imag * cosine], 1)
            bh[c * n1 : (c + 1) * n1], bl[c * n1 : (c + 1) * n1] = split(turned)
        high, low = bh[...], bl[...]
        spec[base] = mm(high, fwdh_ref[...]) + mm(low, fwdh_ref[...]) + mm(high, fwdl_ref[...])

    def synthesize(real, imag):
        high, low = split(jnp.concatenate([real, imag], 1))
        stage = mm(high, bckh_ref[...]) + mm(low, bckh_ref[...]) + mm(high, bckl_ref[...])
        for c in range(mine):
            part = stage[c * n1 : (c + 1) * n1]
            real, imag = part[:, :LANES], part[:, LANES:]
            turned = jnp.concatenate([real * cosine + imag * sine, imag * cosine - real * sine], 0)
            cols = slice(c * LANES, (c + 1) * LANES)
            zh[:, cols], zl[:, cols] = split(turned)
        high, low = zh[...], zl[...]
        result = mm(lasth_ref[...], high) + mm(lasth_ref[...], low) + mm(lastl_ref[...], high)
        for c in range(mine):
            for h in range(folds):
                rows[pl.ds(c * folds + h, shards, stride=mine * folds), :] = result[
                    h * shards : (h + 1) * shards, c * LANES : (c + 1) * LANES
                ]
        return rows[...].reshape(shards, mine * folds, LANES).astype(BF16)

    def parts(k):
        return spec[k, :, :LANES], spec[k, :, LANES:]

    joint(in_send, in_recv, 0).wait_recv()
    analyse(in_recv[:, 0], 0)
    analyse(in_recv[:, 1], 1)
    (sr, si), (fr, fi) = parts(0), parts(1)
    mx_send[...] = synthesize(sr * fr - si * fi, sr * fi + si * fr)
    spread(mx_send, mx_recv, 2)

    joint(rs_send, rs_recv, 1).wait_recv()
    total = grad_out[...]
    for k in range(chans - 1):
        total = total + rs_recv[k].astype(F32)
    grad_out[...] = total
    gr_send[...] = to_rows(total * gate_ref[...].astype(F32))
    spread(gr_send, gr_recv, 3)

    joint(mx_send, mx_recv, 2).wait_recv()
    mixed = jnp.concatenate(from_rows(mx_recv[...]), 1)
    ag_send[...] = jnp.transpose(mixed * gate_ref[...].astype(F32)).astype(BF16)
    for k in range(1, chans):
        pltpu.make_async_remote_copy(
            ag_send, ag_recv.at[k - 1], sends.at[4], recvs.at[4],
            device_id=(me, lax.rem(ch + k, chans)), device_id_type=MESH,
        ).start()
    ggrad_ref[...] = grad_out[...] * mixed

    joint(gr_send, gr_recv, 3).wait_recv()
    analyse(gr_recv[...], 2)
    gr, gi = parts(2)
    fr, fi = parts(1)
    rt_send[:, 0] = synthesize(gr * fr + gi * fi, gi * fr - gr * fi)
    sr, si = parts(0)
    gr, gi = parts(2)
    rt_send[:, 1] = synthesize(gr * sr + gi * si, gi * sr - gr * si)
    spread(rt_send, rt_recv, 5)

    def project(block, gathered):
        part = weight_ref[pl.ds(pl.multiple_of(block * wide, wide), wide), :]
        return mm(gathered, part)

    joint(ag_recv, ag_recv, 4).wait_recv()
    total = project(ch, ag_send[...])
    for k in range(1, chans):
        total = total + project(lax.rem(ch + chans - k, chans), ag_recv[k - 1])
    out_ref[...] = total.astype(BF16)

    joint(rt_send, rt_recv, 5).wait_recv()
    for h, value in enumerate(from_rows(rt_recv[:, 0])):
        sgrad_ref[:, h * LANES : (h + 1) * LANES] = value
    for h, value in enumerate(from_rows(rt_recv[:, 1])):
        cols = slice(h * LANES, (h + 1) * LANES)
        tgrad_ref[:, cols] = value * window[:, cols]

    joint(in_send, in_recv, 0).wait_send()
    joint(rs_send, rs_recv, 1).wait_send()
    joint(mx_send, mx_recv, 2).wait_send()
    joint(gr_send, gr_recv, 3).wait_send()
    joint(ag_recv, ag_recv, 4).wait_send()
    joint(rt_send, rt_recv, 5).wait_send()


def store(*refs):
    half = len(refs) // 2
    copies = [
        pltpu.make_async_copy(refs[k], refs[half + k], refs[-1].at[k]) for k in range(half)
    ]
    for copy in copies:
        copy.start()
    for copy in copies:
        copy.wait()


def stored(values):
    away = pl.BlockSpec(memory_space=pl.ANY)
    return pl.pallas_call(
        store,
        out_shape=tuple(jax.ShapeDtypeStruct(x.shape, x.dtype) for x in values),
        in_specs=[away] * len(values),
        out_specs=(pl.BlockSpec(memory_space=pltpu.HBM),) * len(values),
        scratch_shapes=[pltpu.SemaphoreType.DMA((len(values),))],
        compiler_params=pltpu.CompilerParams(vmem_limit_bytes=1 << 20),
    )(*values)


def per_device(shards, chans, consts, signal, gating, filter_taps, decay_rates, out_weight, out_grad):
    wide, span = signal.shape
    folds = span // LANES
    mine = wide // shards
    n1 = shards * folds
    tile = (mine * folds, LANES)
    vmem = pl.BlockSpec(memory_space=pltpu.VMEM)
    away = pl.BlockSpec(memory_space=pltpu.HBM)
    results = pl.pallas_call(
        functools.partial(body, shards, chans),
        out_shape=(
            jax.ShapeDtypeStruct(out_grad.shape, BF16),
            jax.ShapeDtypeStruct(signal.shape, F32),
            jax.ShapeDtypeStruct(signal.shape, F32),
            jax.ShapeDtypeStruct(signal.shape, F32),
        ),
        in_specs=[away] * (6 + len(consts)),
        out_specs=(vmem,) * 4,
        scratch_shapes=[
            pltpu.VMEM((shards, 2, *tile), BF16),
            pltpu.VMEM((shards, 2, *tile), BF16),
            pltpu.VMEM((chans - 1, wide, span), BF16),
            pltpu.VMEM((chans - 1, wide, span), BF16),
            pltpu.VMEM((shards, *tile), BF16),
            pltpu.VMEM((shards, *tile), BF16),
            pltpu.VMEM((shards, *tile), BF16),
            pltpu.VMEM((shards, *tile), BF16),
            pltpu.VMEM((shards, 2, *tile), BF16),
            pltpu.VMEM((shards, 2, *tile), BF16),
            pltpu.VMEM((span, wide), BF16),
            pltpu.VMEM((chans - 1, span, wide), BF16),
            pltpu.VMEM((wide * folds, LANES), F32),
            pltpu.VMEM((wide, span), F32),
            pltpu.VMEM((wide, span), F32),
            pltpu.VMEM((2 * n1, mine * LANES), BF16),
            pltpu.VMEM((mine * n1, 2 * LANES), BF16),
            pltpu.VMEM((mine * n1, 2 * LANES), BF16),
            pltpu.VMEM((3, mine * n1, 2 * LANES), F32),
            pltpu.VMEM((2 * n1, mine * LANES), BF16),
            pltpu.VMEM((2 * n1, mine * LANES), BF16),
            *(pltpu.VMEM(x.shape, x.dtype) for x in (signal, gating, filter_taps)),
            pltpu.VMEM((wide // LANES, LANES), F32),
            *(pltpu.VMEM(x.shape, x.dtype) for x in (out_weight, out_grad, *consts)),
            pltpu.SemaphoreType.DMA((6,)),
            pltpu.SemaphoreType.DMA((6,)),
            pltpu.SemaphoreType.DMA((9,)),
        ],
        compiler_params=pltpu.CompilerParams(collective_id=0, has_side_effects=True, vmem_limit_bytes=24 << 20),
    )(
        *(
            pltpu.with_memory_space_constraint(x, pltpu.HBM)
            for x in (signal, gating, filter_taps, decay_rates.reshape(-1, LANES), out_weight, out_grad)
        ),
        *(pltpu.with_memory_space_constraint(jnp.asarray(x), pltpu.HBM) for x in consts),
    )
    return stored(results)


def solution(mesh):
    shards, chans = mesh.shape["seq"], mesh.shape["chan"]

    def step(signal, gating, filter_taps, decay_rates, out_weight, out_grad):
        consts = tables(shards, signal.shape[1] // shards // LANES)
        return jax.shard_map(
            functools.partial(per_device, shards, chans, consts),
            mesh=mesh,
            in_specs=(
                P("chan", "seq"),
                P("chan", "seq"),
                P("chan", "seq"),
                P("chan"),
                P(None, "chan"),
                P("seq", "chan"),
            ),
            out_specs=(P("seq", "chan"), P("chan", "seq"), P("chan", "seq"), P("chan", "seq")),
            check_vma=False,
        )(signal, gating, filter_taps, decay_rates, out_weight, out_grad)

    return step
```

```python
import functools

import jax
import jax.numpy as jnp
import numpy as np
from jax import lax
from jax.experimental import pallas as pl
from jax.experimental.pallas import tpu as pltpu
from jax.sharding import PartitionSpec as P

F32, BF16 = jnp.float32, jnp.bfloat16
MESH = pl.DeviceIdType.MESH
LANES = 128


def halves(table):
    high = table.astype(BF16)
    return high, (table - high.astype(np.float64)).astype(BF16)


def tables(shards, folds):
    rows = shards * folds
    length = rows * LANES
    freq = 2 * np.arange(rows)[:, None] + 1
    order = np.arange(rows)
    coarse = folds * (order % shards) + order // shards
    angle = 2 * np.pi * (freq * coarse[None, :] % (4 * rows)) / (4 * rows)
    first = np.concatenate([np.cos(angle), -np.sin(angle)], 0)
    fine = np.arange(LANES)
    turn = 2 * np.pi * (freq * fine[None, :]) / (4 * length)
    inner = 2 * np.pi * (fine[:, None] * fine[None, :] % LANES) / LANES
    re, im = np.cos(inner), -np.sin(inner)
    ahead = np.block([[re, im], [-im, re]])
    back = np.block([[re, -im], [im, re]])
    first_high, first_low = halves(first)
    last_high, last_low = halves(first.T / length)
    return (
        np.stack([np.concatenate([first_high, first_low], 1), *halves(ahead), *halves(back)]),
        np.stack([last_high, last_low]),
        np.stack([np.cos(turn), -np.sin(turn)]).astype(np.float32),
    )


def split(value):
    high = value.astype(BF16)
    return high, (value - high.astype(F32)).astype(BF16)


def mm(left, right):
    return jnp.dot(left, right, preferred_element_type=F32)


def body(
    shards, chans,
    sig_hbm, gate_hbm, taps_hbm, decay_hbm, weight_hbm, og_hbm, square_hbm, last_hbm, turn_hbm,
    out_ref, sgrad_ref, ggrad_ref, tgrad_ref,
    in_send, in_recv, rs_send, rs_recv, mx_send, mx_recv, gr_send, gr_recv, rt_send, rt_recv, ag_send, ag_recv,
    rs_relay, partial,
    rows, window, grad_out, xcat, bh, bl, spec, zh, zl,
    sig_ref, gate_ref, taps_ref, decay_ref, weight_ref, og_ref, square_ref, last_ref, turn_ref,
    sends, recvs, loads, come, go,
):
    me, ch = lax.axis_index("seq"), lax.axis_index("chan")
    far = lax.rem(ch + chans // 2, chans)
    mate = ch + 1 - 2 * lax.rem(ch, 2)
    opposite = chans - 1 - ch
    low = ch < chans // 2
    inner = jnp.logical_or(ch == 1, ch == 2)
    centre = jnp.where(low, 2, 1)
    edge = jnp.where(low, chans - 1, 0)
    wide, span = sig_ref.shape
    folds = span // LANES
    mine = wide // shards
    n1 = shards * folds

    arrivals = [
        pltpu.make_async_copy(source, target, loads.at[k])
        for k, (source, target) in enumerate(
            (
                (sig_hbm, sig_ref), (taps_hbm, taps_ref), (og_hbm, og_ref), (weight_hbm, weight_ref),
                (square_hbm, square_ref), (last_hbm, last_ref), (turn_hbm, turn_ref), (gate_hbm, gate_ref), (decay_hbm, decay_ref),
            )
        )
    ]
    for k in (2, 3, 8, 0, 1, 4, 5, 6, 7):
        arrivals[k].start()
    first_ref, fwdh_ref, fwdl_ref, bckh_ref, bckl_ref = (square_ref.at[k] for k in range(5))
    lasth_ref, lastl_ref = last_ref.at[0], last_ref.at[1]

    barrier = pltpu.get_barrier_semaphore()

    def tell(semaphore, seq, chan):
        pl.semaphore_signal(semaphore, inc=1, device_id=(seq, chan), device_id_type=MESH)

    lead = ch == 0

    @pl.when(lead)
    def _():
        for k in range(1, chans):
            tell(barrier, me, k)

    @pl.when(jnp.logical_not(lead))
    def _():
        for k in range(1, chans):

            @pl.when(ch != k)
            def _():
                tell(barrier, me, k)

    def to_rows(value):
        for h in range(folds):
            rows[pl.ds(h, wide, stride=folds), :] = value[:, h * LANES : (h + 1) * LANES]
        return rows[...].reshape(shards, mine * folds, LANES).astype(BF16)

    def from_rows(block):
        rows[...] = block.astype(F32).reshape(wide * folds, LANES)
        return [rows[pl.ds(h, wide, stride=folds), :] for h in range(folds)]

    def spread(source, target, k):
        @pl.loop(0, shards)
        def _(i):
            peer = lax.rem(me + i, shards)
            pltpu.make_async_remote_copy(
                source.at[peer], target.at[me], sends.at[k], recvs.at[k],
                device_id=(peer, far), device_id_type=MESH,
            ).start()

    def joint(source, target, k):
        return pltpu.make_async_remote_copy(
            source, target, sends.at[k], recvs.at[k], device_id=(me, far), device_id_type=MESH
        )

    arrivals[2].wait()
    arrivals[3].wait()

    def share(block):
        part = weight_ref[pl.ds(pl.multiple_of(block * wide, wide), wide), :]
        return lax.dot_general(part, og_ref[...], (((1,), (1,)), ((), ())), preferred_element_type=F32)

    def along(source, target, k, to):
        return pltpu.make_async_remote_copy(
            source, target, sends.at[k], recvs.at[k], device_id=(me, to), device_id_type=MESH
        )

    half = wide // 2
    cuts = [pl.ds(h * half, half) for h in range(2)]
    relayed = share(edge)

    @pl.when(jnp.logical_not(lead))
    def _():
        pl.semaphore_wait(barrier, chans - 1)
        tell(come, me, 0)

    @pl.when(lead)
    def _():
        pl.semaphore_wait(come, chans - 1)

        @pl.loop(1, shards)
        def _(i):
            tell(barrier, lax.rem(me + i, shards), 0)

    @pl.when(jnp.logical_not(inner))
    def _():
        rs_send[2] = relayed.astype(BF16)
        for h, cut in enumerate(cuts):
            along(rs_send.at[2, cut], rs_relay.at[cut], 6 + h, mate).start()

    @pl.when(inner)
    def _():
        partial[...] = relayed

    rs_send[0] = share(mate).astype(BF16)
    along(rs_send.at[0], rs_recv.at[0], 8, mate).start()
    rs_send[1] = share(centre).astype(BF16)

    @pl.when(inner)
    def _():
        along(rs_send.at[1], rs_recv.at[2], 10, centre).start()

    @pl.when(jnp.logical_not(inner))
    def _():
        along(rs_send.at[1], rs_recv.at[1], 9, centre).start()

    arrivals[8].wait()
    place = lax.broadcasted_iota(jnp.int32, (1, span), 1) + me * span
    place = place.astype(F32)
    for i in range(wide // LANES):
        row = decay_ref[i : i + 1, :]
        rate = jnp.transpose(jnp.broadcast_to(row, (LANES, LANES)))
        size = jnp.sqrt(2.0 * rate)
        for h in range(folds):
            cols = slice(h * LANES, (h + 1) * LANES)
            window[i * LANES : (i + 1) * LANES, cols] = jnp.exp(-rate * place[:, cols]) * size

    arrivals[0].wait()
    arrivals[1].wait()
    in_send[:, 0] = to_rows(sig_ref[...].astype(F32))
    in_send[:, 1] = to_rows(taps_ref[...] * window[...])

    @pl.when(inner)
    def _():
        for h, cut in enumerate(cuts):
            along(rs_send.at[2, cut], rs_relay.at[cut], 6 + h, mate).wait_recv()
            rs_send[2, cut] = (partial[cut, :] + rs_relay[cut, :].astype(F32)).astype(BF16)
            along(rs_send.at[2, cut], rs_recv.at[1, cut], 9, edge).start()

    @pl.when(lead)
    def _():
        pl.semaphore_wait(barrier, shards - 1)
        for k in range(1, chans):
            tell(go, me, k)

    @pl.when(jnp.logical_not(lead))
    def _():
        pl.semaphore_wait(go, 1)

    spread(in_send, in_recv, 0)

    grad_out[...] = share(ch).astype(BF16).astype(F32)

    for arrival in arrivals[4:8]:
        arrival.wait()
    cosine, sine = turn_ref[0], turn_ref[1]

    def analyse(block, base):
        rows[...] = block.astype(F32).reshape(wide * folds, LANES)
        for c in range(mine):
            column = jnp.concatenate(
                [rows[pl.ds(c * folds + h, shards, stride=mine * folds), :] for h in range(folds)], 0
            ).astype(BF16)
            cols = slice(c * LANES, (c + 1) * LANES)
            xcat[:n1, cols] = column
            xcat[n1:, cols] = column
        stage = mm(first_ref[...], xcat[...])
        for c in range(mine):
            cols = slice(c * LANES, (c + 1) * LANES)
            real, imag = stage[:n1, cols], stage[n1:, cols]
            turned = jnp.concatenate([real * cosine - imag * sine, real * sine + imag * cosine], 1)
            bh[c * n1 : (c + 1) * n1], bl[c * n1 : (c + 1) * n1] = split(turned)
        high, low = bh[...], bl[...]
        spec[base] = mm(high, fwdh_ref[...]) + mm(low, fwdh_ref[...]) + mm(high, fwdl_ref[...])

    def synthesize(real, imag):
        high, low = split(jnp.concatenate([real, imag], 1))
        stage = mm(high, bckh_ref[...]) + mm(low, bckh_ref[...]) + mm(high, bckl_ref[...])
        for c in range(mine):
            part = stage[c * n1 : (c + 1) * n1]
            real, imag = part[:, :LANES], part[:, LANES:]
            turned = jnp.concatenate([real * cosine + imag * sine, imag * cosine - real * sine], 0)
            cols = slice(c * LANES, (c + 1) * LANES)
            zh[:, cols], zl[:, cols] = split(turned)
        high, low = zh[...], zl[...]
        result = mm(lasth_ref[...], high) + mm(lasth_ref[...], low) + mm(lastl_ref[...], high)
        for c in range(mine):
            for h in range(folds):
                rows[pl.ds(c * folds + h, shards, stride=mine * folds), :] = result[
                    h * shards : (h + 1) * shards, c * LANES : (c + 1) * LANES
                ]
        return rows[...].reshape(shards, mine * folds, LANES).astype(BF16)

    def parts(k):
        return spec[k, :, :LANES], spec[k, :, LANES:]

    along(rs_send.at[0], rs_recv.at[0], 8, mate).wait_recv()
    along(rs_send.at[1], rs_recv.at[1], 9, mate).wait_recv()
    grad_out[...] = grad_out[...] + rs_recv[0].astype(F32) + rs_recv[1].astype(F32)

    @pl.when(inner)
    def _():
        along(rs_send.at[1], rs_recv.at[2], 10, mate).wait_recv()
        grad_out[...] = grad_out[...] + rs_recv[2].astype(F32)

    total = grad_out[...]
    gr_send[...] = to_rows(total * gate_ref[...].astype(F32))
    spread(gr_send, gr_recv, 3)

    joint(in_send, in_recv, 0).wait_recv()
    analyse(in_recv[:, 0], 0)
    analyse(in_recv[:, 1], 1)
    (sr, si), (fr, fi) = parts(0), parts(1)
    mx_send[...] = synthesize(sr * fr - si * fi, sr * fi + si * fr)
    spread(mx_send, mx_recv, 2)

    joint(gr_send, gr_recv, 3).wait_recv()
    analyse(gr_recv[...], 2)
    gr, gi = parts(2)
    fr, fi = parts(1)
    rt_send[0] = synthesize(gr * fr + gi * fi, gi * fr - gr * fi)
    spread(rt_send.at[0], rt_recv.at[0], 5)
    sr, si = parts(0)
    gr, gi = parts(2)
    rt_send[1] = synthesize(gr * sr + gi * si, gi * sr - gr * si)
    spread(rt_send.at[1], rt_recv.at[1], 4)

    joint(mx_send, mx_recv, 2).wait_recv()
    mixed = jnp.concatenate(from_rows(mx_recv[...]), 1)
    ag_send[...] = jnp.transpose(mixed * gate_ref[...].astype(F32)).astype(BF16)
    for h, cut in enumerate(cuts):
        along(ag_send.at[cut], ag_recv.at[1, cut], 11 + h, far).start()

    @pl.when(inner)
    def _():
        along(ag_send, ag_recv.at[2], 14, opposite).start()

    along(ag_send, ag_recv.at[0], 13, mate).start()
    ggrad_ref[...] = grad_out[...] * mixed

    for h, cut in enumerate(cuts):
        along(ag_send.at[cut], ag_recv.at[1, cut], 11 + h, far).wait_recv()

        @pl.when(inner)
        def _():
            along(ag_recv.at[1, cut], ag_recv.at[2, cut], 15, mate).start()

    def project(block, gathered):
        part = weight_ref[pl.ds(pl.multiple_of(block * wide, wide), wide), :]
        return mm(gathered, part)

    total = project(ch, ag_send[...]) + project(far, ag_recv[1])
    along(ag_send, ag_recv.at[0], 13, mate).wait_recv()
    total = total + project(mate, ag_recv[0])

    @pl.when(inner)
    def _():
        along(ag_send, ag_recv.at[2], 14, opposite).wait_recv()

    @pl.when(jnp.logical_not(inner))
    def _():
        along(ag_send, ag_recv.at[2], 15, mate).wait_recv()

    total = total + project(opposite, ag_recv[2])
    out_ref[...] = total.astype(BF16)

    joint(rt_send.at[0], rt_recv.at[0], 5).wait_recv()
    for h, value in enumerate(from_rows(rt_recv[0])):
        sgrad_ref[:, h * LANES : (h + 1) * LANES] = value
    joint(rt_send.at[1], rt_recv.at[1], 4).wait_recv()
    for h, value in enumerate(from_rows(rt_recv[1])):
        cols = slice(h * LANES, (h + 1) * LANES)
        tgrad_ref[:, cols] = value * window[:, cols]

    joint(in_send, in_recv, 0).wait_send()
    along(rs_send.at[0], rs_recv.at[0], 8, mate).wait_send()

    @pl.when(inner)
    def _():
        along(rs_send.at[1], rs_recv.at[2], 10, mate).wait_send()
        along(rs_send.at[2], rs_recv.at[1], 9, mate).wait_send()

    @pl.when(jnp.logical_not(inner))
    def _():
        along(rs_send.at[1], rs_recv.at[1], 9, mate).wait_send()
        for h, cut in enumerate(cuts):
            along(rs_send.at[2, cut], rs_relay.at[cut], 6 + h, mate).wait_send()

    joint(mx_send, mx_recv, 2).wait_send()
    joint(gr_send, gr_recv, 3).wait_send()
    for h, cut in enumerate(cuts):
        along(ag_send.at[cut], ag_recv.at[1, cut], 11 + h, far).wait_send()
    along(ag_send, ag_recv.at[0], 13, mate).wait_send()

    @pl.when(inner)
    def _():
        along(ag_send, ag_recv.at[2], 14, mate).wait_send()
        along(ag_recv.at[1], ag_recv.at[2], 15, mate).wait_send()

    joint(rt_send.at[0], rt_recv.at[0], 5).wait_send()
    joint(rt_send.at[1], rt_recv.at[1], 4).wait_send()


def store(*refs):
    half = len(refs) // 2
    copies = [
        pltpu.make_async_copy(refs[k], refs[half + k], refs[-1].at[k]) for k in range(half)
    ]
    for copy in copies:
        copy.start()
    for copy in copies:
        copy.wait()


def stored(values):
    away = pl.BlockSpec(memory_space=pl.ANY)
    return pl.pallas_call(
        store,
        out_shape=tuple(jax.ShapeDtypeStruct(x.shape, x.dtype) for x in values),
        in_specs=[away] * len(values),
        out_specs=(pl.BlockSpec(memory_space=pltpu.HBM),) * len(values),
        scratch_shapes=[pltpu.SemaphoreType.DMA((len(values),))],
        compiler_params=pltpu.CompilerParams(vmem_limit_bytes=1 << 20),
    )(*values)


def per_device(shards, chans, consts, signal, gating, filter_taps, decay_rates, out_weight, out_grad):
    wide, span = signal.shape
    folds = span // LANES
    mine = wide // shards
    n1 = shards * folds
    tile = (mine * folds, LANES)
    vmem = pl.BlockSpec(memory_space=pltpu.VMEM)
    away = pl.BlockSpec(memory_space=pltpu.HBM)
    results = pl.pallas_call(
        functools.partial(body, shards, chans),
        out_shape=(
            jax.ShapeDtypeStruct(out_grad.shape, BF16),
            jax.ShapeDtypeStruct(signal.shape, F32),
            jax.ShapeDtypeStruct(signal.shape, F32),
            jax.ShapeDtypeStruct(signal.shape, F32),
        ),
        in_specs=[away] * (6 + len(consts)),
        out_specs=(vmem,) * 4,
        scratch_shapes=[
            pltpu.VMEM((shards, 2, *tile), BF16),
            pltpu.VMEM((shards, 2, *tile), BF16),
            pltpu.VMEM((chans - 1, wide, span), BF16),
            pltpu.VMEM((chans - 1, wide, span), BF16),
            pltpu.VMEM((shards, *tile), BF16),
            pltpu.VMEM((shards, *tile), BF16),
            pltpu.VMEM((shards, *tile), BF16),
            pltpu.VMEM((shards, *tile), BF16),
            pltpu.VMEM((2, shards, *tile), BF16),
            pltpu.VMEM((2, shards, *tile), BF16),
            pltpu.VMEM((span, wide), BF16),
            pltpu.VMEM((chans - 1, span, wide), BF16),
            pltpu.VMEM((wide, span), BF16),
            pltpu.VMEM((wide, span), F32),
            pltpu.VMEM((wide * folds, LANES), F32),
            pltpu.VMEM((wide, span), F32),
            pltpu.VMEM((wide, span), F32),
            pltpu.VMEM((2 * n1, mine * LANES), BF16),
            pltpu.VMEM((mine * n1, 2 * LANES), BF16),
            pltpu.VMEM((mine * n1, 2 * LANES), BF16),
            pltpu.VMEM((3, mine * n1, 2 * LANES), F32),
            pltpu.VMEM((2 * n1, mine * LANES), BF16),
            pltpu.VMEM((2 * n1, mine * LANES), BF16),
            *(pltpu.VMEM(x.shape, x.dtype) for x in (signal, gating, filter_taps)),
            pltpu.VMEM((wide // LANES, LANES), F32),
            *(pltpu.VMEM(x.shape, x.dtype) for x in (out_weight, out_grad, *consts)),
            pltpu.SemaphoreType.DMA((16,)),
            pltpu.SemaphoreType.DMA((16,)),
            pltpu.SemaphoreType.DMA((9,)),
            pltpu.SemaphoreType.REGULAR,
            pltpu.SemaphoreType.REGULAR,
        ],
        compiler_params=pltpu.CompilerParams(collective_id=0, has_side_effects=True, vmem_limit_bytes=24 << 20),
    )(
        *(
            pltpu.with_memory_space_constraint(x, pltpu.HBM)
            for x in (signal, gating, filter_taps, decay_rates.reshape(-1, LANES), out_weight, out_grad)
        ),
        *(pltpu.with_memory_space_constraint(jnp.asarray(x), pltpu.HBM) for x in consts),
    )
    return stored(results)


def solution(mesh):
    shards, chans = mesh.shape["seq"], mesh.shape["chan"]

    def step(signal, gating, filter_taps, decay_rates, out_weight, out_grad):
        consts = tables(shards, signal.shape[1] // shards // LANES)
        return jax.shard_map(
            functools.partial(per_device, shards, chans, consts),
            mesh=mesh,
            in_specs=(
                P("chan", "seq"),
                P("chan", "seq"),
                P("chan", "seq"),
                P("chan"),
                P(None, "chan"),
                P("seq", "chan"),
            ),
            out_specs=(P("seq", "chan"), P("chan", "seq"), P("chan", "seq"), P("chan", "seq")),
            check_vma=False,
        )(signal, gating, filter_taps, decay_rates, out_weight, out_grad)

    return step
```

```python
import functools

import jax
import jax.numpy as jnp
import numpy as np
from jax import lax
from jax.experimental import pallas as pl
from jax.experimental.pallas import tpu as pltpu
from jax.sharding import PartitionSpec as P

F32, BF16 = jnp.float32, jnp.bfloat16
MESH = pl.DeviceIdType.MESH
LANES = 128


def halves(table):
    high = table.astype(BF16)
    return high, (table - high.astype(np.float64)).astype(BF16)


def tables(shards, folds):
    rows = shards * folds
    length = rows * LANES
    freq = 2 * np.arange(rows)[:, None] + 1
    order = np.arange(rows)
    coarse = folds * (order % shards) + order // shards
    angle = 2 * np.pi * (freq * coarse[None, :] % (4 * rows)) / (4 * rows)
    first = np.concatenate([np.cos(angle), -np.sin(angle)], 0)
    fine = np.arange(LANES)
    turn = 2 * np.pi * (freq * fine[None, :]) / (4 * length)
    inner = 2 * np.pi * (fine[:, None] * fine[None, :] % LANES) / LANES
    re, im = np.cos(inner), -np.sin(inner)
    ahead = np.block([[re, im], [-im, re]])
    back = np.block([[re, -im], [im, re]])
    first_high, first_low = halves(first)
    last_high, last_low = halves(first.T / length)
    return (
        np.stack([np.concatenate([first_high, first_low], 1), *halves(ahead), *halves(back)]),
        np.stack([last_high, last_low]),
        np.stack([np.cos(turn), -np.sin(turn)]).astype(np.float32),
    )


def split(value):
    high = value.astype(BF16)
    return high, (value - high.astype(F32)).astype(BF16)


def mm(left, right):
    return jnp.dot(left, right, preferred_element_type=F32)


def body(
    shards, chans,
    sig_hbm, gate_hbm, taps_hbm, decay_hbm, weight_hbm, og_hbm, square_hbm, last_hbm, turn_hbm,
    out_ref, sgrad_ref, ggrad_ref, tgrad_ref,
    in_send, in_recv, rs_send, rs_recv, mx_send, mx_recv, gr_send, gr_recv, rt_send, rt_recv, ag_send, ag_recv,
    rs_relay, partial,
    rows, window, grad_out, xcat, bh, bl, spec, zh, zl,
    sig_ref, gate_ref, taps_ref, decay_ref, weight_ref, og_ref, square_ref, last_ref, turn_ref,
    sends, recvs, loads, come, go,
):
    me, ch = lax.axis_index("seq"), lax.axis_index("chan")
    far = lax.rem(ch + chans // 2, chans)
    mate = ch + 1 - 2 * lax.rem(ch, 2)
    opposite = chans - 1 - ch
    low = ch < chans // 2
    inner = jnp.logical_or(ch == 1, ch == 2)
    centre = jnp.where(low, 2, 1)
    edge = jnp.where(low, chans - 1, 0)
    wide, span = sig_ref.shape
    folds = span // LANES
    mine = wide // shards
    n1 = shards * folds

    arrivals = [
        pltpu.make_async_copy(source, target, loads.at[k])
        for k, (source, target) in enumerate(
            (
                (sig_hbm, sig_ref), (taps_hbm, taps_ref), (og_hbm, og_ref), (weight_hbm, weight_ref),
                (square_hbm, square_ref), (last_hbm, last_ref), (turn_hbm, turn_ref), (gate_hbm, gate_ref), (decay_hbm, decay_ref),
            )
        )
    ]
    for k in (2, 3, 8, 0, 1, 4, 5, 6, 7):
        arrivals[k].start()
    first_ref, fwdh_ref, fwdl_ref, bckh_ref, bckl_ref = (square_ref.at[k] for k in range(5))
    lasth_ref, lastl_ref = last_ref.at[0], last_ref.at[1]

    barrier = pltpu.get_barrier_semaphore()

    def tell(semaphore, seq, chan):
        pl.semaphore_signal(semaphore, inc=1, device_id=(seq, chan), device_id_type=MESH)

    lead = ch == 1
    others = [k for k in range(chans) if k != 1]

    @pl.when(lead)
    def _():
        for k in others:
            tell(barrier, me, k)

    @pl.when(jnp.logical_not(lead))
    def _():
        for k in others:

            @pl.when(ch != k)
            def _():
                tell(barrier, me, k)

    def to_rows(value):
        for h in range(folds):
            rows[pl.ds(h, wide, stride=folds), :] = value[:, h * LANES : (h + 1) * LANES]
        return rows[...].reshape(shards, mine * folds, LANES).astype(BF16)

    def from_rows(block):
        rows[...] = block.astype(F32).reshape(wide * folds, LANES)
        return [rows[pl.ds(h, wide, stride=folds), :] for h in range(folds)]

    def spread(source, target, k):
        @pl.loop(0, shards)
        def _(i):
            peer = lax.rem(me + i, shards)
            pltpu.make_async_remote_copy(
                source.at[peer], target.at[me], sends.at[k], recvs.at[k],
                device_id=(peer, far), device_id_type=MESH,
            ).start()

    def joint(source, target, k):
        return pltpu.make_async_remote_copy(
            source, target, sends.at[k], recvs.at[k], device_id=(me, far), device_id_type=MESH
        )

    arrivals[2].wait()
    arrivals[3].wait()

    def share(block):
        part = weight_ref[pl.ds(pl.multiple_of(block * wide, wide), wide), :]
        return lax.dot_general(part, og_ref[...], (((1,), (1,)), ((), ())), preferred_element_type=F32)

    def along(source, target, k, to):
        return pltpu.make_async_remote_copy(
            source, target, sends.at[k], recvs.at[k], device_id=(me, to), device_id_type=MESH
        )

    half = wide // 2
    cuts = [pl.ds(h * half, half) for h in range(2)]
    relayed = share(edge)

    @pl.when(jnp.logical_not(lead))
    def _():
        pl.semaphore_wait(barrier, chans - 1)
        tell(come, me, 1)

    @pl.when(lead)
    def _():
        pl.semaphore_wait(come, chans - 1)

        @pl.loop(1, shards)
        def _(i):
            tell(barrier, lax.rem(me + i, shards), 1)

    @pl.when(jnp.logical_not(inner))
    def _():
        rs_send[2] = relayed.astype(BF16)
        for h, cut in enumerate(cuts):
            along(rs_send.at[2, cut], rs_relay.at[cut], 6 + h, mate).start()

    @pl.when(inner)
    def _():
        partial[...] = relayed

    rs_send[0] = share(mate).astype(BF16)
    along(rs_send.at[0], rs_recv.at[0], 8, mate).start()
    rs_send[1] = share(centre).astype(BF16)

    @pl.when(inner)
    def _():
        along(rs_send.at[1], rs_recv.at[2], 10, centre).start()

    @pl.when(jnp.logical_not(inner))
    def _():
        along(rs_send.at[1], rs_recv.at[1], 9, centre).start()

    arrivals[8].wait()
    place = lax.broadcasted_iota(jnp.int32, (1, span), 1) + me * span
    place = place.astype(F32)
    for i in range(wide // LANES):
        row = decay_ref[i : i + 1, :]
        rate = jnp.transpose(jnp.broadcast_to(row, (LANES, LANES)))
        size = jnp.sqrt(2.0 * rate)
        for h in range(folds):
            cols = slice(h * LANES, (h + 1) * LANES)
            window[i * LANES : (i + 1) * LANES, cols] = jnp.exp(-rate * place[:, cols]) * size

    arrivals[0].wait()
    arrivals[1].wait()
    in_send[:, 0] = to_rows(sig_ref[...].astype(F32))
    in_send[:, 1] = to_rows(taps_ref[...] * window[...])

    @pl.when(inner)
    def _():
        for h, cut in enumerate(cuts):
            along(rs_send.at[2, cut], rs_relay.at[cut], 6 + h, mate).wait_recv()
            rs_send[2, cut] = (partial[cut, :] + rs_relay[cut, :].astype(F32)).astype(BF16)
            along(rs_send.at[2, cut], rs_recv.at[1, cut], 9, edge).start()

    @pl.when(lead)
    def _():
        pl.semaphore_wait(barrier, shards - 1)
        for k in others:
            tell(go, me, k)

    @pl.when(jnp.logical_not(lead))
    def _():
        pl.semaphore_wait(go, 1)

    spread(in_send, in_recv, 0)

    grad_out[...] = share(ch).astype(BF16).astype(F32)

    for arrival in arrivals[4:8]:
        arrival.wait()
    cosine, sine = turn_ref[0], turn_ref[1]

    def analyse(block, base):
        rows[...] = block.astype(F32).reshape(wide * folds, LANES)
        for c in range(mine):
            column = jnp.concatenate(
                [rows[pl.ds(c * folds + h, shards, stride=mine * folds), :] for h in range(folds)], 0
            ).astype(BF16)
            cols = slice(c * LANES, (c + 1) * LANES)
            xcat[:n1, cols] = column
            xcat[n1:, cols] = column
        stage = mm(first_ref[...], xcat[...])
        for c in range(mine):
            cols = slice(c * LANES, (c + 1) * LANES)
            real, imag = stage[:n1, cols], stage[n1:, cols]
            turned = jnp.concatenate([real * cosine - imag * sine, real * sine + imag * cosine], 1)
            bh[c * n1 : (c + 1) * n1], bl[c * n1 : (c + 1) * n1] = split(turned)
        high, low = bh[...], bl[...]
        spec[base] = mm(high, fwdh_ref[...]) + mm(low, fwdh_ref[...]) + mm(high, fwdl_ref[...])

    def synthesize(real, imag):
        high, low = split(jnp.concatenate([real, imag], 1))
        stage = mm(high, bckh_ref[...]) + mm(low, bckh_ref[...]) + mm(high, bckl_ref[...])
        for c in range(mine):
            part = stage[c * n1 : (c + 1) * n1]
            real, imag = part[:, :LANES], part[:, LANES:]
            turned = jnp.concatenate([real * cosine + imag * sine, imag * cosine - real * sine], 0)
            cols = slice(c * LANES, (c + 1) * LANES)
            zh[:, cols], zl[:, cols] = split(turned)
        high, low = zh[...], zl[...]
        result = mm(lasth_ref[...], high) + mm(lasth_ref[...], low) + mm(lastl_ref[...], high)
        for c in range(mine):
            for h in range(folds):
                rows[pl.ds(c * folds + h, shards, stride=mine * folds), :] = result[
                    h * shards : (h + 1) * shards, c * LANES : (c + 1) * LANES
                ]
        return rows[...].reshape(shards, mine * folds, LANES).astype(BF16)

    def parts(k):
        return spec[k, :, :LANES], spec[k, :, LANES:]

    along(rs_send.at[0], rs_recv.at[0], 8, mate).wait_recv()
    along(rs_send.at[1], rs_recv.at[1], 9, mate).wait_recv()
    grad_out[...] = grad_out[...] + rs_recv[0].astype(F32) + rs_recv[1].astype(F32)

    @pl.when(inner)
    def _():
        along(rs_send.at[1], rs_recv.at[2], 10, mate).wait_recv()
        grad_out[...] = grad_out[...] + rs_recv[2].astype(F32)

    total = grad_out[...]
    gr_send[...] = to_rows(total * gate_ref[...].astype(F32))
    joint(in_send, in_recv, 0).wait_send()
    spread(gr_send, gr_recv, 3)

    joint(in_send, in_recv, 0).wait_recv()
    analyse(in_recv[:, 0], 0)
    analyse(in_recv[:, 1], 1)
    (sr, si), (fr, fi) = parts(0), parts(1)
    mx_send[...] = synthesize(sr * fr - si * fi, sr * fi + si * fr)
    spread(mx_send, mx_recv, 2)

    joint(gr_send, gr_recv, 3).wait_recv()
    analyse(gr_recv[...], 2)
    gr, gi = parts(2)
    fr, fi = parts(1)
    rt_send[0] = synthesize(gr * fr + gi * fi, gi * fr - gr * fi)
    spread(rt_send.at[0], rt_recv.at[0], 5)
    sr, si = parts(0)
    gr, gi = parts(2)
    rt_send[1] = synthesize(gr * sr + gi * si, gi * sr - gr * si)
    spread(rt_send.at[1], rt_recv.at[1], 4)

    joint(mx_send, mx_recv, 2).wait_recv()
    mixed = jnp.concatenate(from_rows(mx_recv[...]), 1)
    ag_send[...] = jnp.transpose(mixed * gate_ref[...].astype(F32)).astype(BF16)
    for h, cut in enumerate(cuts):
        along(ag_send.at[cut], ag_recv.at[1, cut], 11 + h, far).start()

    @pl.when(inner)
    def _():
        along(ag_send, ag_recv.at[2], 14, opposite).start()

    along(ag_send, ag_recv.at[0], 13, mate).start()
    ggrad_ref[...] = grad_out[...] * mixed

    for h, cut in enumerate(cuts):
        along(ag_send.at[cut], ag_recv.at[1, cut], 11 + h, far).wait_recv()

        @pl.when(inner)
        def _():
            along(ag_recv.at[1, cut], ag_recv.at[2, cut], 15, mate).start()

    def project(block, gathered):
        part = weight_ref[pl.ds(pl.multiple_of(block * wide, wide), wide), :]
        return mm(gathered, part)

    total = project(ch, ag_send[...]) + project(far, ag_recv[1])
    along(ag_send, ag_recv.at[0], 13, mate).wait_recv()
    total = total + project(mate, ag_recv[0])

    @pl.when(inner)
    def _():
        along(ag_send, ag_recv.at[2], 14, opposite).wait_recv()

    @pl.when(jnp.logical_not(inner))
    def _():
        along(ag_send, ag_recv.at[2], 15, mate).wait_recv()

    total = total + project(opposite, ag_recv[2])
    out_ref[...] = total.astype(BF16)

    joint(rt_send.at[0], rt_recv.at[0], 5).wait_recv()
    for h, value in enumerate(from_rows(rt_recv[0])):
        sgrad_ref[:, h * LANES : (h + 1) * LANES] = value
    joint(rt_send.at[1], rt_recv.at[1], 4).wait_recv()
    for h, value in enumerate(from_rows(rt_recv[1])):
        cols = slice(h * LANES, (h + 1) * LANES)
        tgrad_ref[:, cols] = value * window[:, cols]

    along(rs_send.at[0], rs_recv.at[0], 8, mate).wait_send()

    @pl.when(inner)
    def _():
        along(rs_send.at[1], rs_recv.at[2], 10, mate).wait_send()
        along(rs_send.at[2], rs_recv.at[1], 9, mate).wait_send()

    @pl.when(jnp.logical_not(inner))
    def _():
        along(rs_send.at[1], rs_recv.at[1], 9, mate).wait_send()
        for h, cut in enumerate(cuts):
            along(rs_send.at[2, cut], rs_relay.at[cut], 6 + h, mate).wait_send()

    joint(mx_send, mx_recv, 2).wait_send()
    joint(gr_send, gr_recv, 3).wait_send()
    for h, cut in enumerate(cuts):
        along(ag_send.at[cut], ag_recv.at[1, cut], 11 + h, far).wait_send()
    along(ag_send, ag_recv.at[0], 13, mate).wait_send()

    @pl.when(inner)
    def _():
        along(ag_send, ag_recv.at[2], 14, mate).wait_send()
        along(ag_recv.at[1], ag_recv.at[2], 15, mate).wait_send()

    joint(rt_send.at[0], rt_recv.at[0], 5).wait_send()
    joint(rt_send.at[1], rt_recv.at[1], 4).wait_send()


def store(*refs):
    half = len(refs) // 2
    copies = [
        pltpu.make_async_copy(refs[k], refs[half + k], refs[-1].at[k]) for k in range(half)
    ]
    for copy in copies:
        copy.start()
    for copy in copies:
        copy.wait()


def stored(values):
    away = pl.BlockSpec(memory_space=pl.ANY)
    return pl.pallas_call(
        store,
        out_shape=tuple(jax.ShapeDtypeStruct(x.shape, x.dtype) for x in values),
        in_specs=[away] * len(values),
        out_specs=(pl.BlockSpec(memory_space=pltpu.HBM),) * len(values),
        scratch_shapes=[pltpu.SemaphoreType.DMA((len(values),))],
        compiler_params=pltpu.CompilerParams(vmem_limit_bytes=1 << 20),
    )(*values)


def per_device(shards, chans, consts, signal, gating, filter_taps, decay_rates, out_weight, out_grad):
    wide, span = signal.shape
    folds = span // LANES
    mine = wide // shards
    n1 = shards * folds
    tile = (mine * folds, LANES)
    vmem = pl.BlockSpec(memory_space=pltpu.VMEM)
    away = pl.BlockSpec(memory_space=pltpu.HBM)
    results = pl.pallas_call(
        functools.partial(body, shards, chans),
        out_shape=(
            jax.ShapeDtypeStruct(out_grad.shape, BF16),
            jax.ShapeDtypeStruct(signal.shape, F32),
            jax.ShapeDtypeStruct(signal.shape, F32),
            jax.ShapeDtypeStruct(signal.shape, F32),
        ),
        in_specs=[away] * (6 + len(consts)),
        out_specs=(vmem,) * 4,
        scratch_shapes=[
            pltpu.VMEM((shards, 2, *tile), BF16),
            pltpu.VMEM((shards, 2, *tile), BF16),
            pltpu.VMEM((chans - 1, wide, span), BF16),
            pltpu.VMEM((chans - 1, wide, span), BF16),
            pltpu.VMEM((shards, *tile), BF16),
            pltpu.VMEM((shards, *tile), BF16),
            pltpu.VMEM((shards, *tile), BF16),
            pltpu.VMEM((shards, *tile), BF16),
            pltpu.VMEM((2, shards, *tile), BF16),
            pltpu.VMEM((2, shards, *tile), BF16),
            pltpu.VMEM((span, wide), BF16),
            pltpu.VMEM((chans - 1, span, wide), BF16),
            pltpu.VMEM((wide, span), BF16),
            pltpu.VMEM((wide, span), F32),
            pltpu.VMEM((wide * folds, LANES), F32),
            pltpu.VMEM((wide, span), F32),
            pltpu.VMEM((wide, span), F32),
            pltpu.VMEM((2 * n1, mine * LANES), BF16),
            pltpu.VMEM((mine * n1, 2 * LANES), BF16),
            pltpu.VMEM((mine * n1, 2 * LANES), BF16),
            pltpu.VMEM((3, mine * n1, 2 * LANES), F32),
            pltpu.VMEM((2 * n1, mine * LANES), BF16),
            pltpu.VMEM((2 * n1, mine * LANES), BF16),
            *(pltpu.VMEM(x.shape, x.dtype) for x in (signal, gating, filter_taps)),
            pltpu.VMEM((wide // LANES, LANES), F32),
            *(pltpu.VMEM(x.shape, x.dtype) for x in (out_weight, out_grad, *consts)),
            pltpu.SemaphoreType.DMA((16,)),
            pltpu.SemaphoreType.DMA((16,)),
            pltpu.SemaphoreType.DMA((9,)),
            pltpu.SemaphoreType.REGULAR,
            pltpu.SemaphoreType.REGULAR,
        ],
        compiler_params=pltpu.CompilerParams(collective_id=0, has_side_effects=True, vmem_limit_bytes=24 << 20),
    )(
        *(
            pltpu.with_memory_space_constraint(x, pltpu.HBM)
            for x in (signal, gating, filter_taps, decay_rates.reshape(-1, LANES), out_weight, out_grad)
        ),
        *(pltpu.with_memory_space_constraint(jnp.asarray(x), pltpu.HBM) for x in consts),
    )
    return stored(results)


def solution(mesh):
    shards, chans = mesh.shape["seq"], mesh.shape["chan"]

    def step(signal, gating, filter_taps, decay_rates, out_weight, out_grad):
        consts = tables(shards, signal.shape[1] // shards // LANES)
        return jax.shard_map(
            functools.partial(per_device, shards, chans, consts),
            mesh=mesh,
            in_specs=(
                P("chan", "seq"),
                P("chan", "seq"),
                P("chan", "seq"),
                P("chan"),
                P(None, "chan"),
                P("seq", "chan"),
            ),
            out_specs=(P("seq", "chan"), P("chan", "seq"), P("chan", "seq"), P("chan", "seq")),
            check_vma=False,
        )(signal, gating, filter_taps, decay_rates, out_weight, out_grad)

    return step
```

```python
import functools

import jax
import jax.numpy as jnp
import numpy as np
from jax import lax
from jax.experimental import pallas as pl
from jax.experimental.pallas import tpu as pltpu
from jax.sharding import PartitionSpec as P

F32, BF16 = jnp.float32, jnp.bfloat16
MESH = pl.DeviceIdType.MESH
LANES = 128


def halves(table):
    high = table.astype(BF16)
    return high, (table - high.astype(np.float64)).astype(BF16)


def tables(shards, folds):
    rows = shards * folds
    length = rows * LANES
    freq = 2 * np.arange(rows)[:, None] + 1
    order = np.arange(rows)
    coarse = folds * (order % shards) + order // shards
    angle = 2 * np.pi * (freq * coarse[None, :] % (4 * rows)) / (4 * rows)
    first = np.concatenate([np.cos(angle), -np.sin(angle)], 0)
    fine = np.arange(LANES)
    turn = 2 * np.pi * (freq * fine[None, :]) / (4 * length)
    inner = 2 * np.pi * (fine[:, None] * fine[None, :] % LANES) / LANES
    re, im = np.cos(inner), -np.sin(inner)
    ahead = np.block([[re, im], [-im, re]])
    back = np.block([[re, -im], [im, re]])
    first_high, first_low = halves(first)
    last_high, last_low = halves(first.T / length)
    return (
        np.stack([np.concatenate([first_high, first_low], 1), *halves(ahead), *halves(back)]),
        np.stack([last_high, last_low]),
        np.stack([np.cos(turn), -np.sin(turn)]).astype(np.float32),
    )


def split(value):
    high = value.astype(BF16)
    return high, (value - high.astype(F32)).astype(BF16)


def mm(left, right):
    return jnp.dot(left, right, preferred_element_type=F32)


def body(
    shards, chans,
    sig_hbm, gate_hbm, taps_hbm, decay_hbm, weight_hbm, og_hbm, square_hbm, last_hbm, turn_hbm,
    out_ref, sgrad_ref, ggrad_ref, tgrad_ref,
    in_send, in_recv, rs_send, rs_recv, mx_send, mx_recv, gr_send, gr_recv, rt_send, rt_recv, ag_send, ag_recv,
    rs_relay, partial,
    rows, window, grad_out, xcat, bh, bl, spec, zh, zl,
    sig_ref, gate_ref, taps_ref, decay_ref, weight_ref, og_ref, square_ref, last_ref, turn_ref,
    sends, recvs, loads, come, go,
):
    me, ch = lax.axis_index("seq"), lax.axis_index("chan")
    far = lax.rem(ch + chans // 2, chans)
    mate = ch + 1 - 2 * lax.rem(ch, 2)
    opposite = chans - 1 - ch
    low = ch < chans // 2
    inner = jnp.logical_or(ch == 1, ch == 2)
    centre = jnp.where(low, 2, 1)
    edge = jnp.where(low, chans - 1, 0)
    wide, span = sig_ref.shape
    folds = span // LANES
    mine = wide // shards
    n1 = shards * folds

    arrivals = [
        pltpu.make_async_copy(source, target, loads.at[k])
        for k, (source, target) in enumerate(
            (
                (sig_hbm, sig_ref), (taps_hbm, taps_ref), (og_hbm, og_ref), (weight_hbm, weight_ref),
                (square_hbm, square_ref), (last_hbm, last_ref), (turn_hbm, turn_ref), (gate_hbm, gate_ref), (decay_hbm, decay_ref),
            )
        )
    ]
    for k in (2, 3, 8, 0, 1, 4, 5, 6, 7):
        arrivals[k].start()
    first_ref, fwdh_ref, fwdl_ref, bckh_ref, bckl_ref = (square_ref.at[k] for k in range(5))
    lasth_ref, lastl_ref = last_ref.at[0], last_ref.at[1]

    barrier = pltpu.get_barrier_semaphore()

    def tell(semaphore, seq, chan):
        pl.semaphore_signal(semaphore, inc=1, device_id=(seq, chan), device_id_type=MESH)

    lead = ch == 1
    others = [k for k in range(chans) if k != 1]

    @pl.when(lead)
    def _():
        for k in others:
            tell(barrier, me, k)

    @pl.when(jnp.logical_not(lead))
    def _():
        for k in others:

            @pl.when(ch != k)
            def _():
                tell(barrier, me, k)

    group = wide // 2
    pair = mine // 2

    def piece(g, h):
        return slice(g * group, (g + 1) * group), slice(h * LANES, (h + 1) * LANES)

    def to_rows(pieces):
        for k, value in enumerate(pieces):
            rows[pl.ds(k, group, stride=2 * folds), :] = value
        return rows[...].reshape(shards, mine * folds, LANES).astype(BF16)

    def from_rows(block):
        rows[...] = block.astype(F32).reshape(wide * folds, LANES)
        return [
            (piece(g, h), rows[pl.ds(g * folds + h, group, stride=2 * folds), :]) for g in range(2) for h in range(folds)
        ]

    def spread(source, target, k):
        @pl.loop(0, shards)
        def _(i):
            peer = lax.rem(me + i, shards)
            pltpu.make_async_remote_copy(
                source.at[peer], target.at[me], sends.at[k], recvs.at[k],
                device_id=(peer, far), device_id_type=MESH,
            ).start()

    def joint(source, target, k):
        return pltpu.make_async_remote_copy(
            source, target, sends.at[k], recvs.at[k], device_id=(me, far), device_id_type=MESH
        )

    arrivals[2].wait()
    arrivals[3].wait()

    def share(block):
        part = weight_ref[pl.ds(pl.multiple_of(block * wide, wide), wide), :]
        return lax.dot_general(part, og_ref[...], (((1,), (1,)), ((), ())), preferred_element_type=F32)

    def along(source, target, k, to):
        return pltpu.make_async_remote_copy(
            source, target, sends.at[k], recvs.at[k], device_id=(me, to), device_id_type=MESH
        )

    half = wide // 2
    cuts = [pl.ds(h * half, half) for h in range(2)]
    relayed = share(edge)

    @pl.when(jnp.logical_not(lead))
    def _():
        pl.semaphore_wait(barrier, chans - 1)
        tell(come, me, 1)

    @pl.when(lead)
    def _():
        pl.semaphore_wait(come, chans - 1)

        @pl.loop(1, shards)
        def _(i):
            tell(barrier, lax.rem(me + i, shards), 1)

    @pl.when(jnp.logical_not(inner))
    def _():
        rs_send[2] = relayed.astype(BF16)
        for h, cut in enumerate(cuts):
            along(rs_send.at[2, cut], rs_relay.at[cut], 6 + h, mate).start()

    @pl.when(inner)
    def _():
        partial[...] = relayed

    rs_send[0] = share(mate).astype(BF16)
    along(rs_send.at[0], rs_recv.at[0], 8, mate).start()
    rs_send[1] = share(centre).astype(BF16)

    @pl.when(inner)
    def _():
        along(rs_send.at[1], rs_recv.at[2], 10, centre).start()

    @pl.when(jnp.logical_not(inner))
    def _():
        along(rs_send.at[1], rs_recv.at[1], 9, centre).start()

    arrivals[8].wait()
    place = lax.broadcasted_iota(jnp.int32, (1, span), 1) + me * span
    place = place.astype(F32)
    for i in range(wide // LANES):
        row = decay_ref[i : i + 1, :]
        rate = jnp.transpose(jnp.broadcast_to(row, (LANES, LANES)))
        size = jnp.sqrt(2.0 * rate)
        for h in range(folds):
            cols = slice(h * LANES, (h + 1) * LANES)
            window[i * LANES : (i + 1) * LANES, cols] = jnp.exp(-rate * place[:, cols]) * size

    arrivals[0].wait()
    arrivals[1].wait()
    for g in range(2):
        spots = [piece(g, h) for h in range(folds)]
        in_send[g] = to_rows(
            [sig_ref[spot].astype(F32) for spot in spots] + [taps_ref[spot] * window[spot] for spot in spots]
        )

    @pl.when(inner)
    def _():
        for h, cut in enumerate(cuts):
            along(rs_send.at[2, cut], rs_relay.at[cut], 6 + h, mate).wait_recv()
            rs_send[2, cut] = (partial[cut, :] + rs_relay[cut, :].astype(F32)).astype(BF16)
            along(rs_send.at[2, cut], rs_recv.at[1, cut], 9, edge).start()

    @pl.when(lead)
    def _():
        pl.semaphore_wait(barrier, shards - 1)
        for k in others:
            tell(go, me, k)

    @pl.when(jnp.logical_not(lead))
    def _():
        pl.semaphore_wait(go, 1)

    spread(in_send.at[0], in_recv.at[0], 0)
    spread(in_send.at[1], in_recv.at[1], 1)

    grad_out[...] = share(ch).astype(BF16).astype(F32)

    for arrival in arrivals[4:8]:
        arrival.wait()
    cosine, sine = turn_ref[0], turn_ref[1]

    def analyse(block, base):
        rows[...] = block.astype(F32).reshape(wide * folds, LANES)
        for k in range(mine):
            start = (k % pair) * 2 * folds + (k // pair) * folds
            column = jnp.concatenate(
                [rows[pl.ds(start + h, shards, stride=mine * folds), :] for h in range(folds)], 0
            ).astype(BF16)
            cols = slice(k * LANES, (k + 1) * LANES)
            xcat[:n1, cols] = column
            xcat[n1:, cols] = column
        stage = mm(first_ref[...], xcat[...])
        for k in range(mine):
            cols = slice(k * LANES, (k + 1) * LANES)
            real, imag = stage[:n1, cols], stage[n1:, cols]
            turned = jnp.concatenate([real * cosine - imag * sine, real * sine + imag * cosine], 1)
            bh[k * n1 : (k + 1) * n1], bl[k * n1 : (k + 1) * n1] = split(turned)
        high, low = bh[...], bl[...]
        spec[base] = mm(high, fwdh_ref[...]) + mm(low, fwdh_ref[...]) + mm(high, fwdl_ref[...])

    def synthesize(real, imag):
        count = real.shape[0] // n1
        high, low = split(jnp.concatenate([real, imag], 1))
        stage = mm(high, bckh_ref[...]) + mm(low, bckh_ref[...]) + mm(high, bckl_ref[...])
        for k in range(count):
            part = stage[k * n1 : (k + 1) * n1]
            real, imag = part[:, :LANES], part[:, LANES:]
            turned = jnp.concatenate([real * cosine + imag * sine, imag * cosine - real * sine], 0)
            cols = slice(k * LANES, (k + 1) * LANES)
            zh[:, cols], zl[:, cols] = split(turned)
        high, low = zh[:, : count * LANES], zl[:, : count * LANES]
        result = mm(lasth_ref[...], high) + mm(lasth_ref[...], low) + mm(lastl_ref[...], high)
        turns = count // pair
        for k in range(count):
            start = (k % pair) * turns * folds + (k // pair) * folds
            for h in range(folds):
                rows[pl.ds(start + h, shards, stride=count * folds), :] = result[
                    h * shards : (h + 1) * shards, k * LANES : (k + 1) * LANES
                ]
        return rows[: shards * count * folds].reshape(shards, count * folds, LANES).astype(BF16)

    def parts(k, top):
        span_rows = slice(top * pair * n1, (top + 1) * pair * n1)
        return spec[k, span_rows, :LANES], spec[k, span_rows, LANES:]

    def publish(g):
        rows[: group * folds] = mx_recv[g].astype(F32).reshape(group * folds, LANES)
        mixed = jnp.concatenate([rows[pl.ds(h, group, stride=folds), :] for h in range(folds)], 1)
        band = slice(g * group, (g + 1) * group)
        ag_send[g] = jnp.transpose(mixed * gate_ref[band, :].astype(F32)).astype(BF16)
        def outward():
            along(ag_send.at[g], ag_recv.at[g, 1], 16 + g, far).start()

        outward()

        @pl.when(inner)
        def _():
            along(ag_send.at[g], ag_recv.at[g, 2], 18 + g, opposite).start()

        along(ag_send.at[g], ag_recv.at[g, 0], 11 + g, mate).start()
        ggrad_ref[band, :] = grad_out[band, :] * mixed

    along(rs_send.at[0], rs_recv.at[0], 8, mate).wait_recv()
    along(rs_send.at[1], rs_recv.at[1], 9, mate).wait_recv()
    grad_out[...] = grad_out[...] + rs_recv[0].astype(F32) + rs_recv[1].astype(F32)

    @pl.when(inner)
    def _():
        along(rs_send.at[1], rs_recv.at[2], 10, mate).wait_recv()
        grad_out[...] = grad_out[...] + rs_recv[2].astype(F32)

    total = grad_out[...]
    grads = total * gate_ref[...].astype(F32)
    gr_send[...] = to_rows([grads[piece(g, h)] for g in range(2) for h in range(folds)])
    joint(in_send.at[0], in_recv.at[0], 0).wait_send()
    joint(in_send.at[1], in_recv.at[1], 1).wait_send()
    spread(gr_send, gr_recv, 3)

    joint(in_send.at[0], in_recv.at[0], 0).wait_recv()
    analyse(in_recv[0], 0)
    (sr, si), (fr, fi) = parts(0, 0), parts(0, 1)
    mx_send[0] = synthesize(sr * fr - si * fi, sr * fi + si * fr)
    spread(mx_send.at[0], mx_recv.at[0], 2)

    joint(in_send.at[1], in_recv.at[1], 1).wait_recv()
    analyse(in_recv[1], 1)
    (sr, si), (fr, fi) = parts(1, 0), parts(1, 1)
    mx_send[1] = synthesize(sr * fr - si * fi, sr * fi + si * fr)
    spread(mx_send.at[1], mx_recv.at[1], 14)

    joint(gr_send, gr_recv, 3).wait_recv()
    analyse(gr_recv[...], 2)
    for u in range(2):
        terms = []
        for g in range(2):
            (gr, gi), (hr, hi) = parts(2, g), parts(g, 1 - u)
            terms.append((gr * hr + gi * hi, gi * hr - gr * hi))
        rt_send[u] = synthesize(*(jnp.concatenate(pieces, 0) for pieces in zip(*terms)))
        spread(rt_send.at[u], rt_recv.at[u], 5 - u)

    joint(mx_send.at[0], mx_recv.at[0], 2).wait_recv()
    publish(0)

    joint(mx_send.at[1], mx_recv.at[1], 14).wait_recv()
    publish(1)

    @pl.when(inner)
    def _():
        for g in range(2):
            along(ag_send.at[g], ag_recv.at[g, 1], 16 + g, far).wait_recv()
            along(ag_recv.at[g, 1], ag_recv.at[g, 2], 20 + g, mate).start()

    @pl.when(jnp.logical_not(inner))
    def _():
        for g in range(2):
            along(ag_send.at[g], ag_recv.at[g, 1], 16 + g, far).wait_recv()

    def project(g, block, gathered):
        start = pl.multiple_of(block * wide + g * group, group)
        return mm(gathered, weight_ref[pl.ds(start, group), :])

    total = project(0, ch, ag_send[0]) + project(1, ch, ag_send[1])
    for g in range(2):
        along(ag_send.at[g], ag_recv.at[g, 0], 11 + g, mate).wait_recv()
        total = total + project(g, mate, ag_recv[g, 0]) + project(g, far, ag_recv[g, 1])
    for g in range(2):

        @pl.when(inner)
        def _():
            along(ag_send.at[g], ag_recv.at[g, 2], 18 + g, opposite).wait_recv()

        @pl.when(jnp.logical_not(inner))
        def _():
            along(ag_send.at[g], ag_recv.at[g, 2], 20 + g, mate).wait_recv()

        total = total + project(g, opposite, ag_recv[g, 2])
    out_ref[...] = total.astype(BF16)

    joint(rt_send.at[0], rt_recv.at[0], 5).wait_recv()
    for spot, value in from_rows(rt_recv[0]):
        sgrad_ref[spot] = value
    joint(rt_send.at[1], rt_recv.at[1], 4).wait_recv()
    for spot, value in from_rows(rt_recv[1]):
        tgrad_ref[spot] = value * window[spot]

    along(rs_send.at[0], rs_recv.at[0], 8, mate).wait_send()

    @pl.when(inner)
    def _():
        along(rs_send.at[1], rs_recv.at[2], 10, mate).wait_send()
        along(rs_send.at[2], rs_recv.at[1], 9, mate).wait_send()

    @pl.when(jnp.logical_not(inner))
    def _():
        along(rs_send.at[1], rs_recv.at[1], 9, mate).wait_send()
        for h, cut in enumerate(cuts):
            along(rs_send.at[2, cut], rs_relay.at[cut], 6 + h, mate).wait_send()

    joint(mx_send.at[0], mx_recv.at[0], 2).wait_send()
    joint(mx_send.at[1], mx_recv.at[1], 14).wait_send()
    joint(gr_send, gr_recv, 3).wait_send()
    for g in range(2):
        along(ag_send.at[g], ag_recv.at[g, 0], 11 + g, mate).wait_send()
        along(ag_send.at[g], ag_recv.at[g, 1], 16 + g, far).wait_send()

    @pl.when(inner)
    def _():
        for g in range(2):
            along(ag_send.at[g], ag_recv.at[g, 2], 18 + g, opposite).wait_send()
            along(ag_recv.at[g, 1], ag_recv.at[g, 2], 20 + g, mate).wait_send()

    joint(rt_send.at[0], rt_recv.at[0], 5).wait_send()
    joint(rt_send.at[1], rt_recv.at[1], 4).wait_send()


def store(*refs):
    half = len(refs) // 2
    copies = [
        pltpu.make_async_copy(refs[k], refs[half + k], refs[-1].at[k]) for k in range(half)
    ]
    for copy in copies:
        copy.start()
    for copy in copies:
        copy.wait()


def stored(values):
    away = pl.BlockSpec(memory_space=pl.ANY)
    return pl.pallas_call(
        store,
        out_shape=tuple(jax.ShapeDtypeStruct(x.shape, x.dtype) for x in values),
        in_specs=[away] * len(values),
        out_specs=(pl.BlockSpec(memory_space=pltpu.HBM),) * len(values),
        scratch_shapes=[pltpu.SemaphoreType.DMA((len(values),))],
        compiler_params=pltpu.CompilerParams(vmem_limit_bytes=1 << 20),
    )(*values)


def per_device(shards, chans, consts, signal, gating, filter_taps, decay_rates, out_weight, out_grad):
    wide, span = signal.shape
    folds = span // LANES
    mine = wide // shards
    n1 = shards * folds
    tile = (mine * folds, LANES)
    vmem = pl.BlockSpec(memory_space=pltpu.VMEM)
    away = pl.BlockSpec(memory_space=pltpu.HBM)
    results = pl.pallas_call(
        functools.partial(body, shards, chans),
        out_shape=(
            jax.ShapeDtypeStruct(out_grad.shape, BF16),
            jax.ShapeDtypeStruct(signal.shape, F32),
            jax.ShapeDtypeStruct(signal.shape, F32),
            jax.ShapeDtypeStruct(signal.shape, F32),
        ),
        in_specs=[away] * (6 + len(consts)),
        out_specs=(vmem,) * 4,
        scratch_shapes=[
            pltpu.VMEM((2, shards, *tile), BF16),
            pltpu.VMEM((2, shards, *tile), BF16),
            pltpu.VMEM((chans - 1, wide, span), BF16),
            pltpu.VMEM((chans - 1, wide, span), BF16),
            pltpu.VMEM((2, shards, tile[0] // 2, LANES), BF16),
            pltpu.VMEM((2, shards, tile[0] // 2, LANES), BF16),
            pltpu.VMEM((shards, *tile), BF16),
            pltpu.VMEM((shards, *tile), BF16),
            pltpu.VMEM((2, shards, *tile), BF16),
            pltpu.VMEM((2, shards, *tile), BF16),
            pltpu.VMEM((2, span, wide // 2), BF16),
            pltpu.VMEM((2, chans - 1, span, wide // 2), BF16),
            pltpu.VMEM((wide, span), BF16),
            pltpu.VMEM((wide, span), F32),
            pltpu.VMEM((wide * folds, LANES), F32),
            pltpu.VMEM((wide, span), F32),
            pltpu.VMEM((wide, span), F32),
            pltpu.VMEM((2 * n1, mine * LANES), BF16),
            pltpu.VMEM((mine * n1, 2 * LANES), BF16),
            pltpu.VMEM((mine * n1, 2 * LANES), BF16),
            pltpu.VMEM((3, mine * n1, 2 * LANES), F32),
            pltpu.VMEM((2 * n1, mine * LANES), BF16),
            pltpu.VMEM((2 * n1, mine * LANES), BF16),
            *(pltpu.VMEM(x.shape, x.dtype) for x in (signal, gating, filter_taps)),
            pltpu.VMEM((wide // LANES, LANES), F32),
            *(pltpu.VMEM(x.shape, x.dtype) for x in (out_weight, out_grad, *consts)),
            pltpu.SemaphoreType.DMA((22,)),
            pltpu.SemaphoreType.DMA((22,)),
            pltpu.SemaphoreType.DMA((9,)),
            pltpu.SemaphoreType.REGULAR,
            pltpu.SemaphoreType.REGULAR,
        ],
        compiler_params=pltpu.CompilerParams(collective_id=0, has_side_effects=True, vmem_limit_bytes=24 << 20),
    )(
        *(
            pltpu.with_memory_space_constraint(x, pltpu.HBM)
            for x in (signal, gating, filter_taps, decay_rates.reshape(-1, LANES), out_weight, out_grad)
        ),
        *(pltpu.with_memory_space_constraint(jnp.asarray(x), pltpu.HBM) for x in consts),
    )
    return stored(results)


def solution(mesh):
    shards, chans = mesh.shape["seq"], mesh.shape["chan"]

    def step(signal, gating, filter_taps, decay_rates, out_weight, out_grad):
        consts = tables(shards, signal.shape[1] // shards // LANES)
        return jax.shard_map(
            functools.partial(per_device, shards, chans, consts),
            mesh=mesh,
            in_specs=(
                P("chan", "seq"),
                P("chan", "seq"),
                P("chan", "seq"),
                P("chan"),
                P(None, "chan"),
                P("seq", "chan"),
            ),
            out_specs=(P("seq", "chan"), P("chan", "seq"), P("chan", "seq"), P("chan", "seq")),
            check_vma=False,
        )(signal, gating, filter_taps, decay_rates, out_weight, out_grad)

    return step
```

```python
import functools

import jax
import jax.numpy as jnp
import numpy as np
from jax import lax
from jax.experimental import pallas as pl
from jax.experimental.pallas import tpu as pltpu
from jax.sharding import PartitionSpec as P

F32, BF16 = jnp.float32, jnp.bfloat16
MESH = pl.DeviceIdType.MESH
LANES = 128


def halves(table):
    high = table.astype(BF16)
    return high, (table - high.astype(np.float64)).astype(BF16)


def tables(shards, folds):
    rows = shards * folds
    length = rows * LANES
    freq = 2 * np.arange(rows)[:, None] + 1
    order = np.arange(rows)
    coarse = folds * (order % shards) + order // shards
    angle = 2 * np.pi * (freq * coarse[None, :] % (4 * rows)) / (4 * rows)
    first = np.concatenate([np.cos(angle), -np.sin(angle)], 0)
    fine = np.arange(LANES)
    turn = 2 * np.pi * (freq * fine[None, :]) / (4 * length)
    inner = 2 * np.pi * (fine[:, None] * fine[None, :] % LANES) / LANES
    re, im = np.cos(inner), -np.sin(inner)
    ahead = np.block([[re, im], [-im, re]])
    back = np.block([[re, -im], [im, re]])
    first_high, first_low = halves(first)
    last_high, last_low = halves(first.T / length)
    return (
        np.stack([np.concatenate([first_high, first_low], 1), *halves(ahead), *halves(back)]),
        np.stack([last_high, last_low]),
        np.stack([np.cos(turn), -np.sin(turn)]).astype(np.float32),
    )


def split(value):
    high = value.astype(BF16)
    return high, (value - high.astype(F32)).astype(BF16)


def mm(left, right):
    return jnp.dot(left, right, preferred_element_type=F32)


def body(
    shards, chans,
    sig_hbm, gate_hbm, taps_hbm, decay_hbm, weight_hbm, og_hbm, square_hbm, last_hbm, turn_hbm,
    out_ref, sgrad_ref, ggrad_ref, tgrad_ref,
    in_send, in_recv, rs_send, rs_recv, mx_send, mx_recv, gr_send, gr_recv, rt_send, rt_recv, ag_send, ag_recv,
    rs_relay, partial,
    rows, window, grad_out, xcat, bh, bl, spec, zh, zl,
    sig_ref, gate_ref, taps_ref, decay_ref, weight_ref, og_ref, square_ref, last_ref, turn_ref,
    sends, recvs, loads, come, go,
):
    me, ch = lax.axis_index("seq"), lax.axis_index("chan")
    far = lax.rem(ch + chans // 2, chans)
    mate = ch + 1 - 2 * lax.rem(ch, 2)
    opposite = chans - 1 - ch
    low = ch < chans // 2
    inner = jnp.logical_or(ch == 1, ch == 2)
    centre = jnp.where(low, 2, 1)
    edge = jnp.where(low, chans - 1, 0)
    wide, span = sig_ref.shape
    folds = span // LANES
    mine = wide // shards
    n1 = shards * folds

    arrivals = [
        pltpu.make_async_copy(source, target, loads.at[k])
        for k, (source, target) in enumerate(
            (
                (sig_hbm, sig_ref), (taps_hbm, taps_ref), (og_hbm, og_ref), (weight_hbm, weight_ref),
                (square_hbm, square_ref), (last_hbm, last_ref), (turn_hbm, turn_ref), (gate_hbm, gate_ref), (decay_hbm, decay_ref),
            )
        )
    ]
    for k in (2, 3, 8, 0, 1, 4, 5, 6, 7):
        arrivals[k].start()
    first_ref, fwdh_ref, fwdl_ref, bckh_ref, bckl_ref = (square_ref.at[k] for k in range(5))
    lasth_ref, lastl_ref = last_ref.at[0], last_ref.at[1]

    barrier = pltpu.get_barrier_semaphore()

    def tell(semaphore, seq, chan):
        pl.semaphore_signal(semaphore, inc=1, device_id=(seq, chan), device_id_type=MESH)

    lead = ch == 1
    others = [k for k in range(chans) if k != 1]

    @pl.when(lead)
    def _():
        for k in others:
            tell(barrier, me, k)

    @pl.when(jnp.logical_not(lead))
    def _():
        for k in others:

            @pl.when(ch != k)
            def _():
                tell(barrier, me, k)

    group = wide // 2
    pair = mine // 2

    def piece(g, h):
        return slice(g * group, (g + 1) * group), slice(h * LANES, (h + 1) * LANES)

    def to_rows(pieces):
        for k, value in enumerate(pieces):
            rows[pl.ds(k, group, stride=2 * folds), :] = value
        return rows[...].reshape(shards, mine * folds, LANES).astype(BF16)

    def from_rows(block):
        rows[...] = block.astype(F32).reshape(wide * folds, LANES)
        return [
            (piece(g, h), rows[pl.ds(g * folds + h, group, stride=2 * folds), :]) for g in range(2) for h in range(folds)
        ]

    def spread(source, target, k):
        @pl.loop(0, shards)
        def _(i):
            peer = lax.rem(me + i, shards)
            pltpu.make_async_remote_copy(
                source.at[peer], target.at[me], sends.at[k], recvs.at[k],
                device_id=(peer, far), device_id_type=MESH,
            ).start()

    def joint(source, target, k):
        return pltpu.make_async_remote_copy(
            source, target, sends.at[k], recvs.at[k], device_id=(me, far), device_id_type=MESH
        )

    arrivals[2].wait()
    arrivals[3].wait()

    def share(block):
        part = weight_ref[pl.ds(pl.multiple_of(block * wide, wide), wide), :]
        return lax.dot_general(part, og_ref[...], (((1,), (1,)), ((), ())), preferred_element_type=F32)

    def along(source, target, k, to):
        return pltpu.make_async_remote_copy(
            source, target, sends.at[k], recvs.at[k], device_id=(me, to), device_id_type=MESH
        )

    half = wide // 2
    cuts = [pl.ds(h * half, half) for h in range(2)]
    relayed = share(edge)

    @pl.when(jnp.logical_not(lead))
    def _():
        pl.semaphore_wait(barrier, chans - 1)
        tell(come, me, 1)

    @pl.when(lead)
    def _():
        pl.semaphore_wait(come, chans - 1)

        @pl.loop(1, shards)
        def _(i):
            tell(barrier, lax.rem(me + i, shards), 1)

    @pl.when(jnp.logical_not(inner))
    def _():
        rs_send[2] = relayed.astype(BF16)
        for h, cut in enumerate(cuts):
            along(rs_send.at[2, cut], rs_relay.at[cut], 6 + h, mate).start()

    @pl.when(inner)
    def _():
        partial[...] = relayed

    rs_send[0] = share(mate).astype(BF16)
    along(rs_send.at[0], rs_recv.at[0], 8, mate).start()
    rs_send[1] = share(centre).astype(BF16)

    @pl.when(inner)
    def _():
        along(rs_send.at[1], rs_recv.at[2], 10, centre).start()

    @pl.when(jnp.logical_not(inner))
    def _():
        along(rs_send.at[1], rs_recv.at[1], 9, centre).start()

    arrivals[8].wait()
    place = lax.broadcasted_iota(jnp.int32, (1, span), 1) + me * span
    place = place.astype(F32)
    for i in range(wide // LANES):
        row = decay_ref[i : i + 1, :]
        rate = jnp.transpose(jnp.broadcast_to(row, (LANES, LANES)))
        size = jnp.sqrt(2.0 * rate)
        for h in range(folds):
            cols = slice(h * LANES, (h + 1) * LANES)
            window[i * LANES : (i + 1) * LANES, cols] = jnp.exp(-rate * place[:, cols]) * size

    arrivals[0].wait()
    arrivals[1].wait()
    for g in range(2):
        spots = [piece(g, h) for h in range(folds)]
        in_send[g] = to_rows(
            [sig_ref[spot].astype(F32) for spot in spots] + [taps_ref[spot] * window[spot] for spot in spots]
        )

    @pl.when(inner)
    def _():
        for h, cut in enumerate(cuts):
            along(rs_send.at[2, cut], rs_relay.at[cut], 6 + h, mate).wait_recv()
            rs_send[2, cut] = (partial[cut, :] + rs_relay[cut, :].astype(F32)).astype(BF16)
            along(rs_send.at[2, cut], rs_recv.at[1, cut], 9, edge).start()

    @pl.when(lead)
    def _():
        pl.semaphore_wait(barrier, shards - 1)
        for k in others:
            tell(go, me, k)

    @pl.when(jnp.logical_not(lead))
    def _():
        pl.semaphore_wait(go, 1)

    spread(in_send.at[0], in_recv.at[0], 0)
    spread(in_send.at[1], in_recv.at[1], 1)

    grad_out[...] = share(ch).astype(BF16).astype(F32)

    for arrival in arrivals[4:8]:
        arrival.wait()
    cosine, sine = turn_ref[0], turn_ref[1]

    def analyse(block, base):
        rows[...] = block.astype(F32).reshape(wide * folds, LANES)
        for k in range(mine):
            start = (k % pair) * 2 * folds + (k // pair) * folds
            column = jnp.concatenate(
                [rows[pl.ds(start + h, shards, stride=mine * folds), :] for h in range(folds)], 0
            ).astype(BF16)
            cols = slice(k * LANES, (k + 1) * LANES)
            xcat[:n1, cols] = column
            xcat[n1:, cols] = column
        stage = mm(first_ref[...], xcat[...])
        for k in range(mine):
            cols = slice(k * LANES, (k + 1) * LANES)
            real, imag = stage[:n1, cols], stage[n1:, cols]
            turned = jnp.concatenate([real * cosine - imag * sine, real * sine + imag * cosine], 1)
            bh[k * n1 : (k + 1) * n1] = turned.astype(BF16)
        high = bh[...]
        spec[base] = mm(high, fwdh_ref[...]) + mm(high, fwdl_ref[...])

    def synthesize(real, imag):
        count = real.shape[0] // n1
        high = jnp.concatenate([real, imag], 1).astype(BF16)
        stage = mm(high, bckh_ref[...]) + mm(high, bckl_ref[...])
        for k in range(count):
            part = stage[k * n1 : (k + 1) * n1]
            real, imag = part[:, :LANES], part[:, LANES:]
            turned = jnp.concatenate([real * cosine + imag * sine, imag * cosine - real * sine], 0)
            cols = slice(k * LANES, (k + 1) * LANES)
            zh[:, cols], zl[:, cols] = split(turned)
        high, low = zh[:, : count * LANES], zl[:, : count * LANES]
        result = mm(lasth_ref[...], high) + mm(lasth_ref[...], low) + mm(lastl_ref[...], high)
        turns = count // pair
        for k in range(count):
            start = (k % pair) * turns * folds + (k // pair) * folds
            for h in range(folds):
                rows[pl.ds(start + h, shards, stride=count * folds), :] = result[
                    h * shards : (h + 1) * shards, k * LANES : (k + 1) * LANES
                ]
        return rows[: shards * count * folds].reshape(shards, count * folds, LANES).astype(BF16)

    def parts(k, top):
        span_rows = slice(top * pair * n1, (top + 1) * pair * n1)
        return spec[k, span_rows, :LANES], spec[k, span_rows, LANES:]

    def publish(g):
        rows[: group * folds] = mx_recv[g].astype(F32).reshape(group * folds, LANES)
        mixed = jnp.concatenate([rows[pl.ds(h, group, stride=folds), :] for h in range(folds)], 1)
        band = slice(g * group, (g + 1) * group)
        ag_send[g] = jnp.transpose(mixed * gate_ref[band, :].astype(F32)).astype(BF16)
        def outward():
            along(ag_send.at[g], ag_recv.at[g, 1], 16 + g, far).start()

        outward()

        @pl.when(inner)
        def _():
            along(ag_send.at[g], ag_recv.at[g, 2], 18 + g, opposite).start()

        along(ag_send.at[g], ag_recv.at[g, 0], 11 + g, mate).start()
        ggrad_ref[band, :] = grad_out[band, :] * mixed

    along(rs_send.at[0], rs_recv.at[0], 8, mate).wait_recv()
    along(rs_send.at[1], rs_recv.at[1], 9, mate).wait_recv()
    grad_out[...] = grad_out[...] + rs_recv[0].astype(F32) + rs_recv[1].astype(F32)

    @pl.when(inner)
    def _():
        along(rs_send.at[1], rs_recv.at[2], 10, mate).wait_recv()
        grad_out[...] = grad_out[...] + rs_recv[2].astype(F32)

    total = grad_out[...]
    grads = total * gate_ref[...].astype(F32)
    gr_send[...] = to_rows([grads[piece(g, h)] for g in range(2) for h in range(folds)])
    joint(in_send.at[0], in_recv.at[0], 0).wait_send()
    joint(in_send.at[1], in_recv.at[1], 1).wait_send()
    spread(gr_send, gr_recv, 3)

    joint(in_send.at[0], in_recv.at[0], 0).wait_recv()
    analyse(in_recv[0], 0)
    (sr, si), (fr, fi) = parts(0, 0), parts(0, 1)
    mx_send[0] = synthesize(sr * fr - si * fi, sr * fi + si * fr)
    spread(mx_send.at[0], mx_recv.at[0], 2)

    joint(in_send.at[1], in_recv.at[1], 1).wait_recv()
    analyse(in_recv[1], 1)
    (sr, si), (fr, fi) = parts(1, 0), parts(1, 1)
    mx_send[1] = synthesize(sr * fr - si * fi, sr * fi + si * fr)
    spread(mx_send.at[1], mx_recv.at[1], 14)

    joint(gr_send, gr_recv, 3).wait_recv()
    analyse(gr_recv[...], 2)
    for u in range(2):
        terms = []
        for g in range(2):
            (gr, gi), (hr, hi) = parts(2, g), parts(g, 1 - u)
            terms.append((gr * hr + gi * hi, gi * hr - gr * hi))
        rt_send[u] = synthesize(*(jnp.concatenate(pieces, 0) for pieces in zip(*terms)))
        spread(rt_send.at[u], rt_recv.at[u], 5 - u)

    joint(mx_send.at[0], mx_recv.at[0], 2).wait_recv()
    publish(0)

    joint(mx_send.at[1], mx_recv.at[1], 14).wait_recv()
    publish(1)

    @pl.when(inner)
    def _():
        for g in range(2):
            along(ag_send.at[g], ag_recv.at[g, 1], 16 + g, far).wait_recv()
            along(ag_recv.at[g, 1], ag_recv.at[g, 2], 20 + g, mate).start()

    @pl.when(jnp.logical_not(inner))
    def _():
        for g in range(2):
            along(ag_send.at[g], ag_recv.at[g, 1], 16 + g, far).wait_recv()

    def project(g, block, gathered):
        start = pl.multiple_of(block * wide + g * group, group)
        return mm(gathered, weight_ref[pl.ds(start, group), :])

    joint(rt_send.at[0], rt_recv.at[0], 5).wait_recv()
    for spot, value in from_rows(rt_recv[0]):
        sgrad_ref[spot] = value
    joint(rt_send.at[1], rt_recv.at[1], 4).wait_recv()
    for spot, value in from_rows(rt_recv[1]):
        tgrad_ref[spot] = value * window[spot]

    total = project(0, ch, ag_send[0]) + project(1, ch, ag_send[1])
    for g in range(2):
        along(ag_send.at[g], ag_recv.at[g, 0], 11 + g, mate).wait_recv()
        total = total + project(g, mate, ag_recv[g, 0]) + project(g, far, ag_recv[g, 1])
    for g in range(2):

        @pl.when(inner)
        def _():
            along(ag_send.at[g], ag_recv.at[g, 2], 18 + g, opposite).wait_recv()

        @pl.when(jnp.logical_not(inner))
        def _():
            along(ag_send.at[g], ag_recv.at[g, 2], 20 + g, mate).wait_recv()

        total = total + project(g, opposite, ag_recv[g, 2])
    out_ref[...] = total.astype(BF16)

    along(rs_send.at[0], rs_recv.at[0], 8, mate).wait_send()

    @pl.when(inner)
    def _():
        along(rs_send.at[1], rs_recv.at[2], 10, mate).wait_send()
        along(rs_send.at[2], rs_recv.at[1], 9, mate).wait_send()

    @pl.when(jnp.logical_not(inner))
    def _():
        along(rs_send.at[1], rs_recv.at[1], 9, mate).wait_send()
        for h, cut in enumerate(cuts):
            along(rs_send.at[2, cut], rs_relay.at[cut], 6 + h, mate).wait_send()

    joint(mx_send.at[0], mx_recv.at[0], 2).wait_send()
    joint(mx_send.at[1], mx_recv.at[1], 14).wait_send()
    joint(gr_send, gr_recv, 3).wait_send()
    for g in range(2):
        along(ag_send.at[g], ag_recv.at[g, 0], 11 + g, mate).wait_send()
        along(ag_send.at[g], ag_recv.at[g, 1], 16 + g, far).wait_send()

    @pl.when(inner)
    def _():
        for g in range(2):
            along(ag_send.at[g], ag_recv.at[g, 2], 18 + g, opposite).wait_send()
            along(ag_recv.at[g, 1], ag_recv.at[g, 2], 20 + g, mate).wait_send()

    joint(rt_send.at[0], rt_recv.at[0], 5).wait_send()
    joint(rt_send.at[1], rt_recv.at[1], 4).wait_send()


def store(*refs):
    half = len(refs) // 2
    copies = [
        pltpu.make_async_copy(refs[k], refs[half + k], refs[-1].at[k]) for k in range(half)
    ]
    for copy in copies:
        copy.start()
    for copy in copies:
        copy.wait()


def stored(values):
    away = pl.BlockSpec(memory_space=pl.ANY)
    return pl.pallas_call(
        store,
        out_shape=tuple(jax.ShapeDtypeStruct(x.shape, x.dtype) for x in values),
        in_specs=[away] * len(values),
        out_specs=(pl.BlockSpec(memory_space=pltpu.HBM),) * len(values),
        scratch_shapes=[pltpu.SemaphoreType.DMA((len(values),))],
        compiler_params=pltpu.CompilerParams(vmem_limit_bytes=1 << 20),
    )(*values)


def per_device(shards, chans, consts, signal, gating, filter_taps, decay_rates, out_weight, out_grad):
    wide, span = signal.shape
    folds = span // LANES
    mine = wide // shards
    n1 = shards * folds
    tile = (mine * folds, LANES)
    vmem = pl.BlockSpec(memory_space=pltpu.VMEM)
    away = pl.BlockSpec(memory_space=pltpu.HBM)
    results = pl.pallas_call(
        functools.partial(body, shards, chans),
        out_shape=(
            jax.ShapeDtypeStruct(out_grad.shape, BF16),
            jax.ShapeDtypeStruct(signal.shape, F32),
            jax.ShapeDtypeStruct(signal.shape, F32),
            jax.ShapeDtypeStruct(signal.shape, F32),
        ),
        in_specs=[away] * (6 + len(consts)),
        out_specs=(vmem,) * 4,
        scratch_shapes=[
            pltpu.VMEM((2, shards, *tile), BF16),
            pltpu.VMEM((2, shards, *tile), BF16),
            pltpu.VMEM((chans - 1, wide, span), BF16),
            pltpu.VMEM((chans - 1, wide, span), BF16),
            pltpu.VMEM((2, shards, tile[0] // 2, LANES), BF16),
            pltpu.VMEM((2, shards, tile[0] // 2, LANES), BF16),
            pltpu.VMEM((shards, *tile), BF16),
            pltpu.VMEM((shards, *tile), BF16),
            pltpu.VMEM((2, shards, *tile), BF16),
            pltpu.VMEM((2, shards, *tile), BF16),
            pltpu.VMEM((2, span, wide // 2), BF16),
            pltpu.VMEM((2, chans - 1, span, wide // 2), BF16),
            pltpu.VMEM((wide, span), BF16),
            pltpu.VMEM((wide, span), F32),
            pltpu.VMEM((wide * folds, LANES), F32),
            pltpu.VMEM((wide, span), F32),
            pltpu.VMEM((wide, span), F32),
            pltpu.VMEM((2 * n1, mine * LANES), BF16),
            pltpu.VMEM((mine * n1, 2 * LANES), BF16),
            pltpu.VMEM((mine * n1, 2 * LANES), BF16),
            pltpu.VMEM((3, mine * n1, 2 * LANES), F32),
            pltpu.VMEM((2 * n1, mine * LANES), BF16),
            pltpu.VMEM((2 * n1, mine * LANES), BF16),
            *(pltpu.VMEM(x.shape, x.dtype) for x in (signal, gating, filter_taps)),
            pltpu.VMEM((wide // LANES, LANES), F32),
            *(pltpu.VMEM(x.shape, x.dtype) for x in (out_weight, out_grad, *consts)),
            pltpu.SemaphoreType.DMA((22,)),
            pltpu.SemaphoreType.DMA((22,)),
            pltpu.SemaphoreType.DMA((9,)),
            pltpu.SemaphoreType.REGULAR,
            pltpu.SemaphoreType.REGULAR,
        ],
        compiler_params=pltpu.CompilerParams(collective_id=0, has_side_effects=True, vmem_limit_bytes=24 << 20),
    )(
        *(
            pltpu.with_memory_space_constraint(x, pltpu.HBM)
            for x in (signal, gating, filter_taps, decay_rates.reshape(-1, LANES), out_weight, out_grad)
        ),
        *(pltpu.with_memory_space_constraint(jnp.asarray(x), pltpu.HBM) for x in consts),
    )
    return stored(results)


def solution(mesh):
    shards, chans = mesh.shape["seq"], mesh.shape["chan"]

    def step(signal, gating, filter_taps, decay_rates, out_weight, out_grad):
        consts = tables(shards, signal.shape[1] // shards // LANES)
        return jax.shard_map(
            functools.partial(per_device, shards, chans, consts),
            mesh=mesh,
            in_specs=(
                P("chan", "seq"),
                P("chan", "seq"),
                P("chan", "seq"),
                P("chan"),
                P(None, "chan"),
                P("seq", "chan"),
            ),
            out_specs=(P("seq", "chan"), P("chan", "seq"), P("chan", "seq"), P("chan", "seq")),
            check_vma=False,
        )(signal, gating, filter_taps, decay_rates, out_weight, out_grad)

    return step
```
